128 devices in a mesh: mpo: 8 (over z, x_lo), sec: 16 (over y, x_hi, core).
Axes of the slice: x: 4 (x_hi: 2, x_lo: 2; x = x_hi * 2 + x_lo), y: 4, z: 4, core: 2. Of those that a mesh axis runs over, the one named last changes fastest.
Arguments:
- wavefunction: bfloat16 [2, 128, 512, 512], P(None, 'sec'), may hold values from -6 to 6
- left_env: bfloat16 [16, 128, 512, 512], P('mpo', 'sec'), may hold values from -0.25 to 0.25
- right_env: bfloat16 [16, 128, 512, 512], P('mpo', 'sec'), may hold values from -0.0625 to 0.0625
- block_dims: int32 [128], P('sec'), may hold values from 128 to 512, as said below
- mpo_shift: int32 [16], P('mpo'), may hold values from -1 to 1
Outputs:
- sigma_blocks: bfloat16 [2, 128, 512, 512], P(None, 'sec', 'mpo')
The draws below stay inside these ranges and needn't reach their ends.
Inputs may be any that keep to these rules, and one draw needn't show every extreme that they name: `block_dims`: some block is full.
All inputs are finite; a program needn't handle non-finite values.
Results may differ from the reference program's by a relative error of at most 0.0049.
Values may be sent and summed in bfloat16 or wider, within the bound.
A program may use at most 192 MiB of HBM per device.

```python
import jax
import jax.numpy as jnp
from jax import lax

DB = 512
KV = 2
NSEC_DEV = 8
W = 16
NSEC = 128
N_SEC = 16


def draw_block_dims(key, part):
    first_key, second_key = jax.random.split(key)
    drawn = jax.random.randint(first_key, (NSEC,), DB // 4, DB + 1)
    full_slot = jax.random.randint(second_key, (), 0, NSEC)
    slots = jnp.arange(NSEC)
    return jnp.where(slots == full_slot, DB, drawn).astype(jnp.int32)


def place_ends(values, stream_key, smallest, high):
    dims = values.shape
    place = [jax.random.randint(jax.random.fold_in(stream_key, axis), (), 0, dims[axis]) for axis in range(len(dims))]
    values = values.at[tuple(place)].set(smallest)
    longest = dims.index(max(dims))
    place[longest] = (place[longest] + 1) % dims[longest]
    return values.at[tuple(place)].set(high)


def levels(stream_key, shape, pieces, least, top_value):
    loudness, own = 1.0, jax.random.fold_in(stream_key, 6)
    for axis_at, parts in pieces:
        steps = jnp.exp(jax.random.uniform(jax.random.fold_in(own, axis_at), (parts,), jnp.float32, least / len(pieces), top_value / len(pieces)))
        loudness = loudness * jnp.repeat(steps, shape[axis_at] // parts).reshape([-1 if axis == axis_at else 1 for axis in range(len(shape))])
    return loudness


def bell_draw(own_key, dims, deviation, most, cuts=(), kind=jnp.bfloat16):
    loudness = levels(own_key, dims, cuts, -0.22, 0.18) if cuts else 1.0
    result = jax.random.normal(own_key, dims, jnp.float32) * deviation * loudness
    return jnp.minimum(jnp.maximum(result, -most), most).astype(kind)


def setup_inputs(seed: int = 0) -> dict:
    keys = jax.random.split(jax.random.key(seed), 6)
    return {
        "wavefunction": bell_draw(keys[0], (KV, NSEC, DB, DB), 1.0, 6.0, ((1, 16),)),
        "left_env": bell_draw(keys[1], (W, NSEC, DB, DB), DB ** -0.5, 0.25, ((0, 8), (1, 16))),
        "right_env": bell_draw(keys[2], (W, NSEC, DB, DB), (DB * W) ** -0.5, 0.0625, ((0, 8), (1, 16))),
        "block_dims": draw_block_dims(jax.random.fold_in(keys[5], 71), 0),
        "mpo_shift": place_ends(jax.random.randint(keys[4], (W,), -1, 2), jax.random.fold_in(keys[4], 1), -1, 1).astype(jnp.int32),
    }


def charge_order(blocks):
    trailing = blocks.shape[1:]
    return blocks.reshape((N_SEC, NSEC_DEV) + trailing).swapaxes(0, 1).reshape((NSEC,) + trailing)


def slot_order(blocks):
    trailing = blocks.shape[1:]
    return blocks.reshape((NSEC_DEV, N_SEC) + trailing).swapaxes(0, 1).reshape((NSEC,) + trailing)


def reference(wavefunction, left_env, right_env, block_dims, mpo_shift):
    own_blocks = jnp.moveaxis(wavefunction, 1, 0)
    by_charge = charge_order(own_blocks)
    empty_block = jnp.zeros_like(by_charge[:1])
    from_lower = slot_order(jnp.concatenate([empty_block, by_charge[:-1]], axis=0))
    from_upper = slot_order(jnp.concatenate([by_charge[1:], empty_block], axis=0))
    variants = jnp.stack([from_upper, own_blocks, from_lower])

    def add_row(accumulated, inputs):
        left_row, right_row, change = inputs
        chosen = lax.dynamic_index_in_dim(variants, (change + 1).astype(jnp.int32), 0, keepdims=False)
        left_part = jnp.einsum('sab,skbc->skac', left_row.astype(jnp.float32), chosen.astype(jnp.float32)).astype(jnp.bfloat16)
        contribution = jnp.einsum('skac,scd->skad', left_part.astype(jnp.float32), right_row.astype(jnp.float32))
        return accumulated + contribution, None

    initial = jnp.zeros(own_blocks.shape, jnp.float32)
    accumulated = lax.scan(add_row, initial, (left_env, right_env, mpo_shift))[0]
    positions = jnp.arange(DB, dtype=jnp.int32)
    block_limit = block_dims[:, None, None, None]
    inside = (positions[None, None, :, None] < block_limit) & (positions[None, None, None, :] < block_limit)
    sigma_blocks = jnp.where(inside, accumulated, jnp.zeros_like(accumulated)).astype(jnp.bfloat16)
    return jnp.moveaxis(sigma_blocks, 0, 1)
```

```python
import functools

import jax
import jax.numpy as jnp
from jax import lax
from jax.experimental import pallas as pl
from jax.experimental.pallas import tpu as pltpu
from jax.sharding import PartitionSpec as P

MESH = pl.DeviceIdType.MESH
RING = 4
ENV_RING = 4
CHIP, SIDE, FWD_UP, FWD_DOWN, PAIR, RELAY_UP, RELAY_DOWN, SUM_UP, SUM_DOWN = range(9)
KINDS = 9


def kernel(
    shift_ref, dims_ref, wave_ref, left_ref, right_ref, out_ref,
    own, chip, side, left_buf, right_buf, chosen, parts, pair_send, pair_recv, total,
    relay_send, relay_recv, sum_send, sum_recv,
    send_sem, recv_sem, own_sem, left_sem, right_sem,
):
    slots, block = wave_ref.shape[1], wave_ref.shape[2]
    half = block // 2
    slab = block // 8
    mpo = lax.axis_index("mpo")
    sec = lax.axis_index("sec")
    secs = lax.axis_size("sec")
    core = sec % 2
    z = mpo // 2
    x_lo = mpo % 2
    k_side = z % 2
    up = ((mpo + 2) % 8, sec)
    down = ((mpo + 6) % 8, sec)
    pair = (mpo + 1 - 2 * x_lo, sec)
    chip_mate = (mpo, sec + 1 - 2 * core)
    side_mate = (mpo + 1 - 2 * x_lo, (sec + secs - 1 + 2 * core) % secs)
    first = (secs - 1 - sec) // (secs - 1)
    last = sec // (secs - 1)

    def remote(kind, slot, src, dst, device):
        return pltpu.make_async_remote_copy(
            src_ref=src, dst_ref=dst, send_sem=send_sem.at[kind, slot],
            recv_sem=recv_sem.at[kind, slot], device_id=device, device_id_type=MESH,
        )

    def chip_copy(slot):
        return remote(CHIP, slot, wave_ref.at[:, slot], chip.at[slot], chip_mate)

    def side_copy(slot):
        source = (slot + first - last + slots) % slots
        return remote(SIDE, slot, wave_ref.at[k_side, source], side.at[slot, k_side], side_mate)

    def forward_up(slot, k):
        piece = side.at[slot, k, pl.ds(0, half)]
        return remote(FWD_UP, slot, piece, piece, up)

    def forward_down(slot, k):
        piece = side.at[slot, k, pl.ds(half, half)]
        return remote(FWD_DOWN, slot, piece, piece, down)

    def pair_copy(slot):
        return remote(PAIR, slot, pair_send.at[slot], pair_recv.at[slot], pair)

    def relay_copy(way, slot):
        return remote(RELAY_UP + way, slot, relay_send.at[way, slot], relay_recv.at[way, slot], (up, down)[way])

    def sum_copy(way, slot):
        return remote(SUM_UP + way, slot, sum_send.at[way, slot], sum_recv.at[way, slot], (up, down)[way])

    def own_copy(slot):
        return pltpu.make_async_copy(wave_ref.at[:, slot], own.at[slot], own_sem.at[slot])

    def left_copy(slot):
        at = slot % ENV_RING
        return pltpu.make_async_copy(left_ref.at[:, slot], left_buf.at[at], left_sem.at[at])

    def right_copy(slot):
        at = slot % ENV_RING
        return pltpu.make_async_copy(right_ref.at[:, slot], right_buf.at[at], right_sem.at[at])

    barrier = pltpu.get_barrier_semaphore()
    for mate in (up, down, pair, chip_mate, side_mate):
        pl.semaphore_signal(barrier, inc=1, device_id=mate, device_id_type=MESH)

    def start_local(slot, carry):
        own_copy(slot).start()
        left_copy(slot).start()
        right_copy(slot).start()
        return carry

    lax.fori_loop(0, ENV_RING - 1, start_local, 0)
    pl.semaphore_wait(barrier, 5)

    def start_remote(slot, carry):
        side_copy(slot).start()
        chip_copy(slot).start()
        return carry

    lax.fori_loop(0, slots, start_remote, 0)

    def stage_forward(slot):
        side_copy(slot).wait_recv()
        forward_up(slot, k_side).start()
        forward_down(slot, k_side).start()

    def stage_finish(slot):
        sum_copy(0, slot).wait_recv()
        sum_copy(1, slot).wait_recv()
        limit = dims_ref[slot]
        shape = (2, slab, block)
        rows = mpo * slab + lax.broadcasted_iota(jnp.int32, shape, 1)
        cols = lax.broadcasted_iota(jnp.int32, shape, 2)
        value = total[slot % RING, z] + sum_recv[0, slot].astype(jnp.float32)
        value = value + sum_recv[1, slot].astype(jnp.float32)
        inside = (rows < limit) & (cols < limit)
        out_ref[:, slot] = jnp.where(inside, value, jnp.zeros_like(value)).astype(jnp.bfloat16)

    def stage_sum(slot):
        relay_copy(0, slot).wait_recv()
        relay_copy(1, slot).wait_recv()
        at = slot % RING
        above, below = (z + 1) % 4, (z + 3) % 4
        sum_send[0, slot, 0] = (total[at, above, 0] + relay_recv[0, slot].astype(jnp.float32)).astype(jnp.bfloat16)
        sum_send[0, slot, 1] = total[at, above, 1].astype(jnp.bfloat16)
        sum_send[1, slot, 0] = total[at, below, 0].astype(jnp.bfloat16)
        sum_send[1, slot, 1] = (total[at, below, 1] + relay_recv[1, slot].astype(jnp.float32)).astype(jnp.bfloat16)
        sum_copy(0, slot).start()
        sum_copy(1, slot).start()

    def stage_pair(slot):
        pair_copy(slot).wait_recv()
        at = slot % RING
        total[at] = total[at] + pair_recv[slot].astype(jnp.float32)
        far = (z + 2) % 4
        relay_send[0, slot] = total[at, far, 0].astype(jnp.bfloat16)
        relay_send[1, slot] = total[at, far, 1].astype(jnp.bfloat16)
        relay_copy(0, slot).start()
        relay_copy(1, slot).start()

    def stage_compute(slot):
        at = slot % ENV_RING
        own_copy(slot).wait()
        left_copy(slot).wait()
        right_copy(slot).wait()
        chip_copy(slot).wait_recv()
        forward_up(slot, 1 - k_side).wait_recv()
        forward_down(slot, 1 - k_side).wait_recv()
        missing = first * ((slots - 1 - slot) // (slots - 1)) + last * (slot // (slots - 1))
        for w in range(2):
            turn = shift_ref[w] * (1 - 2 * core)
            use_side = (turn == 1).astype(jnp.float32) * (1 - missing).astype(jnp.float32)
            use_chip = (turn == -1).astype(jnp.float32)
            use_own = (turn == 0).astype(jnp.float32)
            for k in range(2):
                chosen[k] = (
                    own[slot, k] * use_own.astype(jnp.bfloat16)
                    + chip[slot, k] * use_chip.astype(jnp.bfloat16)
                    + side[slot, k] * use_side.astype(jnp.bfloat16)
                )
            theirs = left_buf[at, w, :, 1 - x_lo].reshape(half, block)
            mine = left_buf[at, w, :, x_lo].reshape(half, block)
            rows = jnp.concatenate([theirs, mine], axis=0)
            for k in range(2):
                parts[k, w] = jnp.dot(rows, chosen[k], preferred_element_type=jnp.float32).astype(jnp.bfloat16)
        for k in range(2):
            both = jnp.dot(parts[k, 0], right_buf[at, 0], preferred_element_type=jnp.float32) + jnp.dot(
                parts[k, 1], right_buf[at, 1], preferred_element_type=jnp.float32
            )
            pair_send[slot, :, k] = both[:half].astype(jnp.bfloat16).reshape(4, slab, block)
            total[slot % RING, :, k] = both[half:].reshape(4, slab, block)
        pair_copy(slot).start()

    def step(i, carry):
        @pl.when(i < slots)
        def _():
            stage_forward(i)

        @pl.when(i + ENV_RING - 1 < slots)
        def _():
            start_local(i + ENV_RING - 1, 0)

        @pl.when(i >= 3)
        def _():
            stage_finish(i - 3)

        @pl.when((i >= 2) & (i < slots + 2))
        def _():
            stage_sum(i - 2)

        @pl.when((i >= 1) & (i < slots + 1))
        def _():
            stage_pair(i - 1)

        @pl.when(i < slots)
        def _():
            stage_compute(i)

        return carry

    lax.fori_loop(0, slots + 3, step, 0)

    def drain(slot, carry):
        side_copy(slot).wait_send()
        chip_copy(slot).wait_send()
        forward_up(slot, k_side).wait_send()
        forward_down(slot, k_side).wait_send()
        pair_copy(slot).wait_send()
        for way in range(2):
            relay_copy(way, slot).wait_send()
            sum_copy(way, slot).wait_send()
        return carry

    lax.fori_loop(0, slots, drain, 0)


def body(wavefunction, left_env, right_env, block_dims, mpo_shift):
    vectors, slots, block, _ = wavefunction.shape
    slab = block // 8
    left_env = left_env.reshape(2, slots, 4, 2, slab, block)
    bf16, f32 = jnp.bfloat16, jnp.float32
    smem = pl.BlockSpec(memory_space=pltpu.SMEM)
    anywhere = pl.BlockSpec(memory_space=pl.ANY)
    return pl.pallas_call(
        kernel,
        out_shape=jax.ShapeDtypeStruct((vectors, slots, slab, block), bf16),
        in_specs=[smem, smem, anywhere, anywhere, anywhere],
        out_specs=pl.BlockSpec(memory_space=pltpu.VMEM),
        scratch_shapes=[
            pltpu.VMEM((slots, 2, block, block), bf16),
            pltpu.VMEM((slots, 2, block, block), bf16),
            pltpu.VMEM((slots, 2, block, block), bf16),
            pltpu.VMEM((ENV_RING, 2, 4, 2, slab, block), bf16),
            pltpu.VMEM((ENV_RING, 2, block, block), bf16),
            pltpu.VMEM((2, block, block), bf16),
            pltpu.VMEM((2, 2, block, block), bf16),
            pltpu.VMEM((slots, 4, 2, slab, block), bf16),
            pltpu.VMEM((slots, 4, 2, slab, block), bf16),
            pltpu.VMEM((RING, 4, 2, slab, block), f32),
            pltpu.VMEM((2, slots, slab, block), bf16),
            pltpu.VMEM((2, slots, slab, block), bf16),
            pltpu.VMEM((2, slots, 2, slab, block), bf16),
            pltpu.VMEM((2, slots, 2, slab, block), bf16),
            pltpu.SemaphoreType.DMA((KINDS, slots)),
            pltpu.SemaphoreType.DMA((KINDS, slots)),
            pltpu.SemaphoreType.DMA((slots,)),
            pltpu.SemaphoreType.DMA((ENV_RING,)),
            pltpu.SemaphoreType.DMA((ENV_RING,)),
        ],
        compiler_params=pltpu.CompilerParams(
            collective_id=0, has_side_effects=True, vmem_limit_bytes=66 * 1000 * 1000
        ),
        name="matvec",
    )(mpo_shift, block_dims, wavefunction, left_env, right_env)


def solution(mesh):
    placed = (
        P(None, "sec", None, None),
        P("mpo", "sec", None, None),
        P("mpo", "sec", None, None),
        P("sec"),
        P("mpo"),
    )
    return jax.shard_map(
        body, mesh=mesh, in_specs=placed, out_specs=P(None, "sec", "mpo", None), check_vma=False
    )
```

```python
import functools

import jax
import jax.numpy as jnp
from jax import lax
from jax.experimental import pallas as pl
from jax.experimental.pallas import tpu as pltpu
from jax.sharding import PartitionSpec as P

MESH = pl.DeviceIdType.MESH
LAG = 2
RING = LAG + 3
ENV_RING = 4
CHIP, SIDE, FWD_UP, FWD_DOWN, PAIR, RELAY_UP, RELAY_DOWN, SUM_UP, SUM_DOWN = range(9)
KINDS = 9


def kernel(
    shift_ref, dims_ref, wave_ref, left_ref, right_ref, out_ref,
    own, chip, side, left_buf, right_buf, chosen, parts, pair_send, pair_recv, total,
    relay_send, relay_recv, sum_send, sum_recv,
    send_sem, recv_sem, own_sem, left_sem, right_sem,
):
    slots, block = wave_ref.shape[1], wave_ref.shape[2]
    units = 2 * slots
    half = block // 2
    quarter = block // 4
    slab = block // 8
    mpo = lax.axis_index("mpo")
    sec = lax.axis_index("sec")
    secs = lax.axis_size("sec")
    core = sec % 2
    z = mpo // 2
    x_lo = mpo % 2
    direct = (z % 2) * half
    indirect = half - direct
    up = ((mpo + 2) % 8, sec)
    down = ((mpo + 6) % 8, sec)
    pair = (mpo + 1 - 2 * x_lo, sec)
    chip_mate = (mpo, sec + 1 - 2 * core)
    side_mate = (mpo + 1 - 2 * x_lo, (sec + secs - 1 + 2 * core) % secs)
    first = (secs - 1 - sec) // (secs - 1)
    last = sec // (secs - 1)

    def remote(kind, unit, src, dst, device):
        return pltpu.make_async_remote_copy(
            src_ref=src, dst_ref=dst, send_sem=send_sem.at[kind, unit],
            recv_sem=recv_sem.at[kind, unit], device_id=device, device_id_type=MESH,
        )

    def chip_copy(unit):
        return remote(CHIP, unit, wave_ref.at[unit % 2, unit // 2], chip.at[unit], chip_mate)

    def side_copy(unit):
        source = (unit // 2 + first - last + slots) % slots
        rows = pl.ds(direct, half)
        return remote(SIDE, unit, wave_ref.at[unit % 2, source, rows], side.at[unit, rows], side_mate)

    def forward_up(unit, start):
        piece = side.at[unit, pl.ds(start, quarter)]
        return remote(FWD_UP, unit, piece, piece, up)

    def forward_down(unit, start):
        piece = side.at[unit, pl.ds(start + quarter, quarter)]
        return remote(FWD_DOWN, unit, piece, piece, down)

    def pair_copy(unit):
        return remote(PAIR, unit, pair_send.at[unit], pair_recv.at[unit], pair)

    def relay_copy(way, unit):
        return remote(RELAY_UP + way, unit, relay_send.at[way, unit], relay_recv.at[way, unit], (up, down)[way])

    def sum_copy(way, unit):
        return remote(SUM_UP + way, unit, sum_send.at[way, unit], sum_recv.at[way, unit], (up, down)[way])

    def own_copy(unit):
        return pltpu.make_async_copy(wave_ref.at[unit % 2, unit // 2], own.at[unit], own_sem.at[unit])

    def left_copy(slot):
        at = slot % ENV_RING
        return pltpu.make_async_copy(left_ref.at[:, slot], left_buf.at[at], left_sem.at[at])

    def right_copy(slot):
        at = slot % ENV_RING
        return pltpu.make_async_copy(right_ref.at[:, slot], right_buf.at[at], right_sem.at[at])

    barrier = pltpu.get_barrier_semaphore()
    for mate in (up, down, pair, chip_mate, side_mate):
        pl.semaphore_signal(barrier, inc=1, device_id=mate, device_id_type=MESH)

    def start_local(slot, carry):
        own_copy(2 * slot).start()
        own_copy(2 * slot + 1).start()
        left_copy(slot).start()
        right_copy(slot).start()
        return carry

    lax.fori_loop(0, ENV_RING - 1, start_local, 0)
    pl.semaphore_wait(barrier, 5)

    def start_remote(unit, carry):
        side_copy(unit).start()
        chip_copy(unit).start()
        return carry

    lax.fori_loop(0, units, start_remote, 0)

    def stage_forward(unit):
        side_copy(unit).wait_recv()
        forward_up(unit, direct).start()
        forward_down(unit, direct).start()

    def stage_finish(unit):
        sum_copy(0, unit).wait_recv()
        sum_copy(1, unit).wait_recv()
        limit = dims_ref[unit // 2]
        shape = (slab, block)
        rows = mpo * slab + lax.broadcasted_iota(jnp.int32, shape, 0)
        cols = lax.broadcasted_iota(jnp.int32, shape, 1)
        value = total[unit % RING, z] + sum_recv[0, unit].astype(jnp.float32)
        value = value + sum_recv[1, unit].astype(jnp.float32)
        inside = (rows < limit) & (cols < limit)
        out_ref[unit % 2, unit // 2] = jnp.where(inside, value, jnp.zeros_like(value)).astype(jnp.bfloat16)

    top, bottom = pl.ds(0, slab // 2), pl.ds(slab // 2, slab // 2)

    def stage_sum(unit):
        relay_copy(0, unit).wait_recv()
        relay_copy(1, unit).wait_recv()
        at = unit % RING
        above, below = (z + 1) % 4, (z + 3) % 4
        sum_send[0, unit, top] = (total[at, above, top] + relay_recv[0, unit].astype(jnp.float32)).astype(jnp.bfloat16)
        sum_send[0, unit, bottom] = total[at, above, bottom].astype(jnp.bfloat16)
        sum_send[1, unit, top] = total[at, below, top].astype(jnp.bfloat16)
        sum_send[1, unit, bottom] = (total[at, below, bottom] + relay_recv[1, unit].astype(jnp.float32)).astype(
            jnp.bfloat16
        )
        sum_copy(0, unit).start()
        sum_copy(1, unit).start()

    def stage_pair(unit):
        pair_copy(unit).wait_recv()
        at = unit % RING
        total[at] = total[at] + pair_recv[unit].astype(jnp.float32)
        far = (z + 2) % 4
        relay_send[0, unit] = total[at, far, top].astype(jnp.bfloat16)
        relay_send[1, unit] = total[at, far, bottom].astype(jnp.bfloat16)
        relay_copy(0, unit).start()
        relay_copy(1, unit).start()

    def stage_compute(unit):
        slot = unit // 2
        at = slot % ENV_RING
        own_copy(unit).wait()

        @pl.when(unit % 2 == 0)
        def _():
            left_copy(slot).wait()
            right_copy(slot).wait()

        chip_copy(unit).wait_recv()
        forward_up(unit, indirect).wait_recv()
        forward_down(unit, indirect).wait_recv()
        missing = first * ((slots - 1 - slot) // (slots - 1)) + last * (slot // (slots - 1))
        for w in range(2):
            turn = shift_ref[w] * (1 - 2 * core)
            use_side = (turn == 1).astype(jnp.float32) * (1 - missing).astype(jnp.float32)
            use_chip = (turn == -1).astype(jnp.float32)
            use_own = (turn == 0).astype(jnp.float32)
            chosen[w] = (
                own[unit] * use_own.astype(jnp.bfloat16)
                + chip[unit] * use_chip.astype(jnp.bfloat16)
                + side[unit] * use_side.astype(jnp.bfloat16)
            )
            theirs = left_buf[at, w, :, 1 - x_lo].reshape(half, block)
            mine = left_buf[at, w, :, x_lo].reshape(half, block)
            rows = jnp.concatenate([theirs, mine], axis=0)
            parts[w] = jnp.dot(rows, chosen[w], preferred_element_type=jnp.float32).astype(jnp.bfloat16)
        both = jnp.dot(parts[0], right_buf[at, 0], preferred_element_type=jnp.float32) + jnp.dot(
            parts[1], right_buf[at, 1], preferred_element_type=jnp.float32
        )
        pair_send[unit] = both[:half].astype(jnp.bfloat16).reshape(4, slab, block)
        total[unit % RING] = both[half:].reshape(4, slab, block)
        pair_copy(unit).start()

    def step(i, carry):
        @pl.when(i < units)
        def _():
            stage_forward(i)

        ahead = i // 2 + ENV_RING - 1

        @pl.when((i % 2 == 0) & (ahead < slots))
        def _():
            start_local(ahead, 0)

        @pl.when(i >= LAG + 2)
        def _():
            stage_finish(i - LAG - 2)

        @pl.when((i >= LAG + 1) & (i < units + LAG + 1))
        def _():
            stage_sum(i - LAG - 1)

        @pl.when((i >= LAG) & (i < units + LAG))
        def _():
            stage_pair(i - LAG)

        @pl.when(i < units)
        def _():
            stage_compute(i)

        return carry

    lax.fori_loop(0, units + LAG + 2, step, 0)

    def drain(unit, carry):
        side_copy(unit).wait_send()
        chip_copy(unit).wait_send()
        forward_up(unit, direct).wait_send()
        forward_down(unit, direct).wait_send()
        pair_copy(unit).wait_send()
        for way in range(2):
            relay_copy(way, unit).wait_send()
            sum_copy(way, unit).wait_send()
        return carry

    lax.fori_loop(0, units, drain, 0)


def body(wavefunction, left_env, right_env, block_dims, mpo_shift):
    vectors, slots, block, _ = wavefunction.shape
    slab, units = block // 8, 2 * slots
    left_env = left_env.reshape(2, slots, 4, 2, slab, block)
    bf16, f32 = jnp.bfloat16, jnp.float32
    smem = pl.BlockSpec(memory_space=pltpu.SMEM)
    anywhere = pl.BlockSpec(memory_space=pl.ANY)
    return pl.pallas_call(
        kernel,
        out_shape=jax.ShapeDtypeStruct((vectors, slots, slab, block), bf16),
        in_specs=[smem, smem, anywhere, anywhere, anywhere],
        out_specs=pl.BlockSpec(memory_space=pltpu.VMEM),
        scratch_shapes=[
            pltpu.VMEM((units, block, block), bf16),
            pltpu.VMEM((units, block, block), bf16),
            pltpu.VMEM((units, block, block), bf16),
            pltpu.VMEM((ENV_RING, 2, 4, 2, slab, block), bf16),
            pltpu.VMEM((ENV_RING, 2, block, block), bf16),
            pltpu.VMEM((2, block, block), bf16),
            pltpu.VMEM((2, block, block), bf16),
            pltpu.VMEM((units, 4, slab, block), bf16),
            pltpu.VMEM((units, 4, slab, block), bf16),
            pltpu.VMEM((RING, 4, slab, block), f32),
            pltpu.VMEM((2, units, slab // 2, block), bf16),
            pltpu.VMEM((2, units, slab // 2, block), bf16),
            pltpu.VMEM((2, units, slab, block), bf16),
            pltpu.VMEM((2, units, slab, block), bf16),
            pltpu.SemaphoreType.DMA((KINDS, units)),
            pltpu.SemaphoreType.DMA((KINDS, units)),
            pltpu.SemaphoreType.DMA((units,)),
            pltpu.SemaphoreType.DMA((ENV_RING,)),
            pltpu.SemaphoreType.DMA((ENV_RING,)),
        ],
        compiler_params=pltpu.CompilerParams(
            collective_id=0, has_side_effects=True, vmem_limit_bytes=66 * 1000 * 1000
        ),
        name="matvec",
    )(mpo_shift, block_dims, wavefunction, left_env, right_env)


def solution(mesh):
    placed = (
        P(None, "sec", None, None),
        P("mpo", "sec", None, None),
        P("mpo", "sec", None, None),
        P("sec"),
        P("mpo"),
    )
    return jax.shard_map(
        body, mesh=mesh, in_specs=placed, out_specs=P(None, "sec", "mpo", None), check_vma=False
    )
```

```python
import functools

import jax
import jax.numpy as jnp
from jax import lax
from jax.experimental import pallas as pl
from jax.experimental.pallas import tpu as pltpu
from jax.sharding import PartitionSpec as P

MESH = pl.DeviceIdType.MESH
LAG = 2
TAIL_LAG = 1
RING = LAG + 3
ENV_RING = 4
BY_QUARTER = 5
Z_FIRST = 2
Z_FROM, Z_STEP = 10, 5
CHIP, SIDE, FWD_UP, FWD_DOWN, HOP_UP, HOP_DOWN, RELAY_UP, RELAY_DOWN, SUM_UP, SUM_DOWN = range(10)
PAIR_FAR, PAIR_ABOVE, PAIR_BELOW, PAIR_OWN = range(10, 14)
KINDS = 14


def is_tail(unit):
    return (unit >= Z_FROM) & (unit % Z_STEP == Z_FROM % Z_STEP)


def tail_slot(unit):
    return (unit - Z_FROM) // Z_STEP


def kernel(
    shift_ref, dims_ref, wave_ref, left_ref, right_ref, out_ref,
    own, chip, side, left_buf, right_buf, chosen, parts,
    pair_send, pair_recv, total, relay_send, relay_recv, sum_send, sum_recv,
    tail_total, tail_relay_send, tail_relay_recv, tail_sum_send, tail_sum_recv, tail_pair_send, tail_pair_recv,
    send_sem, recv_sem, own_sem, left_sem, right_sem,
):
    bf16, f32 = jnp.bfloat16, jnp.float32
    slots, block = wave_ref.shape[1], wave_ref.shape[2]
    units = 2 * slots
    half, quarter, eighth = block // 2, block // 4, block // 8
    slab = block // 8
    mpo = lax.axis_index("mpo")
    sec = lax.axis_index("sec")
    secs = lax.axis_size("sec")
    core = sec % 2
    z = mpo // 2
    x_lo = mpo % 2
    above, below, far = (z + 1) % 4, (z + 3) % 4, (z + 2) % 4
    direct = (z % 2) * half
    indirect = half - direct
    up = ((mpo + 2) % 8, sec)
    down = ((mpo + 6) % 8, sec)
    pair = (mpo + 1 - 2 * x_lo, sec)
    chip_mate = (mpo, sec + 1 - 2 * core)
    side_mate = (mpo + 1 - 2 * x_lo, (sec + secs - 1 + 2 * core) % secs)
    first = (secs - 1 - sec) // (secs - 1)
    last = sec // (secs - 1)

    def remote(kind, unit, src, dst, device):
        return pltpu.make_async_remote_copy(
            src_ref=src, dst_ref=dst, send_sem=send_sem.at[kind, unit],
            recv_sem=recv_sem.at[kind, unit], device_id=device, device_id_type=MESH,
        )

    def chip_copy(unit):
        return remote(CHIP, unit, wave_ref.at[unit % 2, unit // 2], chip.at[unit], chip_mate)

    def side_copy(unit, start, size):
        source = (unit // 2 + first - last + slots) % slots
        rows = pl.ds(start, size)
        return remote(SIDE, unit, wave_ref.at[unit % 2, source, rows], side.at[unit, rows], side_mate)

    def pass_on(kind, unit, start, size, device):
        piece = side.at[unit, pl.ds(start, size)]
        return remote(kind, unit, piece, piece, device)

    def half_up(unit, start):
        return pass_on(FWD_UP, unit, start, quarter, up)

    def half_down(unit, start):
        return pass_on(FWD_DOWN, unit, start + quarter, quarter, down)

    def quarter_up(unit, layer):
        return pass_on(FWD_UP, unit, layer * quarter, quarter, up)

    def quarter_down(unit, layer):
        return pass_on(FWD_DOWN, unit, layer * quarter, quarter, down)

    def hop_up(unit, layer):
        return pass_on(HOP_UP, unit, layer * quarter, eighth, up)

    def hop_down(unit, layer):
        return pass_on(HOP_DOWN, unit, layer * quarter + eighth, eighth, down)

    def pair_copy(kind, unit):
        layer = {PAIR_FAR: far, PAIR_ABOVE: above, PAIR_BELOW: below, PAIR_OWN: z}[kind]
        return remote(kind, unit, pair_send.at[unit, layer], pair_recv.at[unit, layer], pair)

    def relay_copy(way, unit):
        return remote(RELAY_UP + way, unit, relay_send.at[way, unit], relay_recv.at[way, unit], (up, down)[way])

    def sum_copy(way, unit):
        return remote(SUM_UP + way, unit, sum_send.at[way, unit], sum_recv.at[way, unit], (up, down)[way])

    def tail_pair_copy(unit):
        at = tail_slot(unit)
        return remote(PAIR_OWN, unit, tail_pair_send.at[at], tail_pair_recv.at[at], pair)

    def tail_relay_copy(way, unit):
        at = tail_slot(unit)
        return remote(
            RELAY_UP + way, unit, tail_relay_send.at[way, at], tail_relay_recv.at[way, at], (up, down)[way]
        )

    def tail_sum_copy(way, unit):
        at = tail_slot(unit)
        return remote(SUM_UP + way, unit, tail_sum_send.at[way, at], tail_sum_recv.at[way, at], (up, down)[way])

    def own_copy(unit):
        return pltpu.make_async_copy(wave_ref.at[unit % 2, unit // 2], own.at[unit], own_sem.at[unit])

    def left_copy(slot):
        at = slot % ENV_RING
        return pltpu.make_async_copy(left_ref.at[:, slot], left_buf.at[at], left_sem.at[at])

    def right_copy(slot):
        at = slot % ENV_RING
        return pltpu.make_async_copy(right_ref.at[:, slot], right_buf.at[at], right_sem.at[at])

    barrier = pltpu.get_barrier_semaphore()
    for mate in (up, down, pair, chip_mate, side_mate):
        pl.semaphore_signal(barrier, inc=1, device_id=mate, device_id_type=MESH)

    def start_local(slot, carry):
        own_copy(2 * slot).start()
        own_copy(2 * slot + 1).start()
        left_copy(slot).start()
        right_copy(slot).start()
        return carry

    lax.fori_loop(0, ENV_RING - 1, start_local, 0)
    pl.semaphore_wait(barrier, 5)

    def start_quarters(unit, carry):
        side_copy(unit, z * quarter, quarter).start()
        chip_copy(unit).start()
        return carry

    def start_halves(unit, carry):
        side_copy(unit, direct, half).start()
        chip_copy(unit).start()
        return carry

    lax.fori_loop(0, BY_QUARTER, start_quarters, 0)
    lax.fori_loop(BY_QUARTER, units, start_halves, 0)

    def stage_quarter(unit):
        side_copy(unit, z * quarter, quarter).wait_recv()
        quarter_up(unit, z).start()
        quarter_down(unit, z).start()

    def stage_hop(unit):
        quarter_up(unit, below).wait_recv()
        hop_up(unit, below).start()
        quarter_down(unit, above).wait_recv()
        hop_down(unit, above).start()

    def stage_half(unit):
        side_copy(unit, direct, half).wait_recv()
        half_up(unit, direct).start()
        half_down(unit, direct).start()

    def write(unit, value):
        limit = dims_ref[unit // 2]
        rows = mpo * slab + lax.broadcasted_iota(jnp.int32, value.shape, 0)
        cols = lax.broadcasted_iota(jnp.int32, value.shape, 1)
        inside = (rows < limit) & (cols < limit)
        out_ref[unit % 2, unit // 2] = jnp.where(inside, value, jnp.zeros_like(value)).astype(bf16)

    top, bottom = pl.ds(0, slab // 2), pl.ds(slab // 2, slab // 2)

    def summed(unit, layer, rows=slice(None)):
        return total[unit % RING, layer, rows] + pair_recv[unit, layer, rows].astype(f32)

    def stage_finish(unit):
        pair_copy(PAIR_OWN, unit).wait_recv()
        sum_copy(0, unit).wait_recv()
        sum_copy(1, unit).wait_recv()
        value = summed(unit, z) + sum_recv[0, unit].astype(f32)
        write(unit, value + sum_recv[1, unit].astype(f32))

    def stage_sum(unit):
        pair_copy(PAIR_ABOVE, unit).wait_recv()
        relay_copy(0, unit).wait_recv()
        sum_send[0, unit, top] = (summed(unit, above, top) + relay_recv[0, unit].astype(f32)).astype(bf16)
        sum_send[0, unit, bottom] = summed(unit, above, bottom).astype(bf16)
        sum_copy(0, unit).start()
        pair_copy(PAIR_BELOW, unit).wait_recv()
        relay_copy(1, unit).wait_recv()
        sum_send[1, unit, top] = summed(unit, below, top).astype(bf16)
        sum_send[1, unit, bottom] = (summed(unit, below, bottom) + relay_recv[1, unit].astype(f32)).astype(bf16)
        sum_copy(1, unit).start()

    def stage_pair(unit):
        pair_copy(PAIR_FAR, unit).wait_recv()
        relay_send[0, unit] = summed(unit, far, top).astype(bf16)
        relay_copy(0, unit).start()
        relay_send[1, unit] = summed(unit, far, bottom).astype(bf16)
        relay_copy(1, unit).start()

    def tail_finish(unit):
        at = tail_slot(unit)
        tail_pair_copy(unit).wait_recv()
        write(unit, tail_total[at, 1, z] + tail_pair_recv[at].astype(f32))

    def tail_pair(unit):
        at = tail_slot(unit)
        tail_sum_copy(0, unit).wait_recv()
        tail_sum_copy(1, unit).wait_recv()
        for side_of in range(2):
            value = tail_total[at, side_of, z] + tail_sum_recv[0, at, side_of].astype(f32)
            value = value + tail_sum_recv[1, at, side_of].astype(f32)
            if side_of == 0:
                tail_pair_send[at] = value.astype(bf16)
                tail_pair_copy(unit).start()
            else:
                tail_total[at, 1, z] = value

    def tail_sum(unit):
        at = tail_slot(unit)
        tail_relay_copy(0, unit).wait_recv()
        tail_sum_send[0, at, 0] = (tail_total[at, 0, above] + tail_relay_recv[0, at].astype(f32)).astype(bf16)
        tail_sum_send[0, at, 1] = tail_total[at, 1, above].astype(bf16)
        tail_sum_copy(0, unit).start()
        tail_relay_copy(1, unit).wait_recv()
        tail_sum_send[1, at, 0] = tail_total[at, 0, below].astype(bf16)
        tail_sum_send[1, at, 1] = (tail_total[at, 1, below] + tail_relay_recv[1, at].astype(f32)).astype(bf16)
        tail_sum_copy(1, unit).start()

    def stage_compute(unit):
        slot = unit // 2
        at = slot % ENV_RING
        own_copy(unit).wait()

        @pl.when(unit % 2 == 0)
        def _():
            left_copy(slot).wait()
            right_copy(slot).wait()

        chip_copy(unit).wait_recv()

        @pl.when(unit < BY_QUARTER)
        def _():
            hop_up(unit, far).wait_recv()
            hop_down(unit, far).wait_recv()

        @pl.when(unit >= BY_QUARTER)
        def _():
            half_up(unit, indirect).wait_recv()
            half_down(unit, indirect).wait_recv()

        missing = first * ((slots - 1 - slot) // (slots - 1)) + last * (slot // (slots - 1))
        for w in range(2):
            turn = shift_ref[w] * (1 - 2 * core)
            use_side = (turn == 1).astype(f32) * (1 - missing).astype(f32)
            use_chip = (turn == -1).astype(f32)
            use_own = (turn == 0).astype(f32)
            chosen[w] = (
                own[unit] * use_own.astype(bf16)
                + chip[unit] * use_chip.astype(bf16)
                + side[unit] * use_side.astype(bf16)
            )
            theirs = left_buf[at, w, :, 1 - x_lo].reshape(half, block)
            mine = left_buf[at, w, :, x_lo].reshape(half, block)
            rows = jnp.concatenate([theirs, mine], axis=0)
            parts[w] = jnp.dot(rows, chosen[w], preferred_element_type=f32).astype(bf16)
        both = jnp.dot(parts[0], right_buf[at, 0], preferred_element_type=f32) + jnp.dot(
            parts[1], right_buf[at, 1], preferred_element_type=f32
        )

        @pl.when(jnp.logical_not(is_tail(unit)))
        def _():
            pair_send[unit] = both[:half].astype(bf16).reshape(4, slab, block)
            for kind in (PAIR_FAR, PAIR_ABOVE, PAIR_BELOW, PAIR_OWN):
                pair_copy(kind, unit).start()
            total[unit % RING] = both[half:].reshape(4, slab, block)

        @pl.when(is_tail(unit))
        def _():
            tail = tail_slot(unit)
            tail_total[tail] = both.reshape(2, 4, slab, block)
            for way in range(2):
                tail_relay_send[way, tail] = tail_total[tail, way, far].astype(bf16)
                tail_relay_copy(way, unit).start()

    def step(i, carry):
        @pl.when(i < BY_QUARTER)
        def _():
            stage_quarter(i)

        @pl.when((i >= BY_QUARTER) & (i < units))
        def _():
            stage_half(i)

        now = i - 2
        ahead = now // 2 + ENV_RING - 1

        @pl.when((now >= 0) & (now % 2 == 0) & (ahead < slots))
        def _():
            start_local(ahead, 0)

        def later(lag, tail, stage):
            unit = now - lag
            kind = is_tail(unit) if tail else jnp.logical_not(is_tail(unit))

            @pl.when((unit >= 0) & (unit < units) & kind)
            def _():
                stage(unit)

        later(LAG + 2, False, stage_finish)
        later(LAG + 1, False, stage_sum)
        later(TAIL_LAG + 2, True, tail_finish)
        later(LAG, False, stage_pair)
        later(TAIL_LAG + 1, True, tail_pair)
        later(TAIL_LAG, True, tail_sum)

        @pl.when((i >= 1) & (i < BY_QUARTER + 1))
        def _():
            stage_hop(i - 1)

        @pl.when((now >= 0) & (now < units))
        def _():
            stage_compute(now)

        return carry

    lax.fori_loop(0, 2 + units + LAG + 2, step, 0)

    def drain_quarters(unit, carry):
        side_copy(unit, z * quarter, quarter).wait_send()
        quarter_up(unit, z).wait_send()
        quarter_down(unit, z).wait_send()
        hop_up(unit, below).wait_send()
        hop_down(unit, above).wait_send()
        return carry

    def drain_halves(unit, carry):
        side_copy(unit, direct, half).wait_send()
        half_up(unit, direct).wait_send()
        half_down(unit, direct).wait_send()
        return carry

    def drain_sums(unit, carry):
        chip_copy(unit).wait_send()

        @pl.when(jnp.logical_not(is_tail(unit)))
        def _():
            for kind in (PAIR_FAR, PAIR_ABOVE, PAIR_BELOW, PAIR_OWN):
                pair_copy(kind, unit).wait_send()
            for way in range(2):
                relay_copy(way, unit).wait_send()
                sum_copy(way, unit).wait_send()

        @pl.when(is_tail(unit))
        def _():
            tail_pair_copy(unit).wait_send()
            for way in range(2):
                tail_relay_copy(way, unit).wait_send()
                tail_sum_copy(way, unit).wait_send()

        return carry

    lax.fori_loop(0, BY_QUARTER, drain_quarters, 0)
    lax.fori_loop(BY_QUARTER, units, drain_halves, 0)
    lax.fori_loop(0, units, drain_sums, 0)


def body(wavefunction, left_env, right_env, block_dims, mpo_shift):
    vectors, slots, block, _ = wavefunction.shape
    slab, units = block // 8, 2 * slots
    left_env = left_env.reshape(2, slots, 4, 2, slab, block)
    bf16, f32 = jnp.bfloat16, jnp.float32
    smem = pl.BlockSpec(memory_space=pltpu.SMEM)
    anywhere = pl.BlockSpec(memory_space=pl.ANY)
    return pl.pallas_call(
        kernel,
        out_shape=jax.ShapeDtypeStruct((vectors, slots, slab, block), bf16),
        in_specs=[smem, smem, anywhere, anywhere, anywhere],
        out_specs=pl.BlockSpec(memory_space=pltpu.VMEM),
        scratch_shapes=[
            pltpu.VMEM((units, block, block), bf16),
            pltpu.VMEM((units, block, block), bf16),
            pltpu.VMEM((units, block, block), bf16),
            pltpu.VMEM((ENV_RING, 2, 4, 2, slab, block), bf16),
            pltpu.VMEM((ENV_RING, 2, block, block), bf16),
            pltpu.VMEM((2, block, block), bf16),
            pltpu.VMEM((2, block, block), bf16),
            pltpu.VMEM((units, 4, slab, block), bf16),
            pltpu.VMEM((units, 4, slab, block), bf16),
            pltpu.VMEM((RING, 4, slab, block), f32),
            pltpu.VMEM((2, units, slab // 2, block), bf16),
            pltpu.VMEM((2, units, slab // 2, block), bf16),
            pltpu.VMEM((2, units, slab, block), bf16),
            pltpu.VMEM((2, units, slab, block), bf16),
            pltpu.VMEM((Z_FIRST, 2, 4, slab, block), f32),
            pltpu.VMEM((2, Z_FIRST, slab, block), bf16),
            pltpu.VMEM((2, Z_FIRST, slab, block), bf16),
            pltpu.VMEM((2, Z_FIRST, 2, slab, block), bf16),
            pltpu.VMEM((2, Z_FIRST, 2, slab, block), bf16),
            pltpu.VMEM((Z_FIRST, slab, block), bf16),
            pltpu.VMEM((Z_FIRST, slab, block), bf16),
            pltpu.SemaphoreType.DMA((KINDS, units)),
            pltpu.SemaphoreType.DMA((KINDS, units)),
            pltpu.SemaphoreType.DMA((units,)),
            pltpu.SemaphoreType.DMA((ENV_RING,)),
            pltpu.SemaphoreType.DMA((ENV_RING,)),
        ],
        compiler_params=pltpu.CompilerParams(
            collective_id=0, has_side_effects=True, vmem_limit_bytes=66 * 1000 * 1000
        ),
        name="matvec",
    )(mpo_shift, block_dims, wavefunction, left_env, right_env)


def solution(mesh):
    placed = (
        P(None, "sec", None, None),
        P("mpo", "sec", None, None),
        P("mpo", "sec", None, None),
        P("sec"),
        P("mpo"),
    )
    return jax.shard_map(
        body, mesh=mesh, in_specs=placed, out_specs=P(None, "sec", "mpo", None), check_vma=False
    )
```

```python
import functools

import jax
import jax.numpy as jnp
from jax import lax
from jax.experimental import pallas as pl
from jax.experimental.pallas import tpu as pltpu
from jax.sharding import PartitionSpec as P

MESH = pl.DeviceIdType.MESH
LAGS = (2, 4, 5)
TAIL_LAGS = (1, 3, 4)
AHEAD = 2
RING = max(LAGS) + 1
ENV_RING = 4
BY_QUARTER = (0, 1, 2, 3, 4, 10, 12)
WHOLE = (11, 15)
Z_FIRST = (8, 13, 15)
Z_SLOTS = next(n for n in range(len(Z_FIRST), 17) if len({u % n for u in Z_FIRST}) == len(Z_FIRST))
CHIP, SIDE, FWD_UP, FWD_DOWN, HOP_UP, HOP_DOWN, RELAY_UP, RELAY_DOWN, SUM_UP, SUM_DOWN = range(10)
PAIR_FAR, PAIR_ABOVE, PAIR_BELOW, PAIR_OWN = range(10, 14)
KINDS = 14


def one_of(unit, members):
    found = unit == members[0]
    for member in members[1:]:
        found = found | (unit == member)
    return found


def is_tail(unit):
    return one_of(unit, Z_FIRST)


def tail_slot(unit):
    return unit % Z_SLOTS


def kernel(
    shift_ref, dims_ref, wave_ref, left_ref, right_ref, out_ref,
    own, chip, side, left_buf, right_buf, chosen, parts,
    pair_send, pair_recv, total, relay_send, relay_recv, sum_send, sum_recv,
    tail_total, tail_relay_send, tail_relay_recv, tail_sum_send, tail_sum_recv, tail_pair_send, tail_pair_recv,
    out_buf, send_sem, recv_sem, own_sem, left_sem, right_sem, out_sem,
):
    bf16, f32 = jnp.bfloat16, jnp.float32
    slots, block = wave_ref.shape[1], wave_ref.shape[2]
    units = 2 * slots
    half, quarter, eighth = block // 2, block // 4, block // 8
    slab = block // 8
    mpo = lax.axis_index("mpo")
    sec = lax.axis_index("sec")
    secs = lax.axis_size("sec")
    core = sec % 2
    z = mpo // 2
    x_lo = mpo % 2
    above, below, far = (z + 1) % 4, (z + 3) % 4, (z + 2) % 4
    direct = (z % 2) * half
    indirect = half - direct
    up = ((mpo + 2) % 8, sec)
    down = ((mpo + 6) % 8, sec)
    pair = (mpo + 1 - 2 * x_lo, sec)
    chip_mate = (mpo, sec + 1 - 2 * core)
    side_mate = (mpo + 1 - 2 * x_lo, (sec + secs - 1 + 2 * core) % secs)
    first = (secs - 1 - sec) // (secs - 1)
    last = sec // (secs - 1)

    def remote(kind, unit, src, dst, device):
        return pltpu.make_async_remote_copy(
            src_ref=src, dst_ref=dst, send_sem=send_sem.at[kind, unit],
            recv_sem=recv_sem.at[kind, unit], device_id=device, device_id_type=MESH,
        )

    def chip_copy(unit):
        return remote(CHIP, unit, wave_ref.at[unit % 2, unit // 2], chip.at[unit], chip_mate)

    def side_copy(unit, start, size):
        source = (unit // 2 + first - last + slots) % slots
        rows = pl.ds(start, size)
        return remote(SIDE, unit, wave_ref.at[unit % 2, source, rows], side.at[unit, rows], side_mate)

    def pass_on(kind, unit, start, size, device):
        piece = side.at[unit, pl.ds(start, size)]
        return remote(kind, unit, piece, piece, device)

    def half_up(unit, start):
        return pass_on(FWD_UP, unit, start, quarter, up)

    def half_down(unit, start):
        return pass_on(FWD_DOWN, unit, start + quarter, quarter, down)

    def quarter_up(unit, layer):
        return pass_on(FWD_UP, unit, layer * quarter, quarter, up)

    def quarter_down(unit, layer):
        return pass_on(FWD_DOWN, unit, layer * quarter, quarter, down)

    def hop_up(unit, layer):
        return pass_on(HOP_UP, unit, layer * quarter, eighth, up)

    def hop_down(unit, layer):
        return pass_on(HOP_DOWN, unit, layer * quarter + eighth, eighth, down)

    def pair_copy(kind, unit):
        layer = {PAIR_FAR: far, PAIR_ABOVE: above, PAIR_BELOW: below, PAIR_OWN: z}[kind]
        return remote(kind, unit, pair_send.at[unit, layer], pair_recv.at[unit, layer], pair)

    def relay_copy(way, unit):
        return remote(RELAY_UP + way, unit, relay_send.at[way, unit], relay_recv.at[way, unit], (up, down)[way])

    def sum_copy(way, unit):
        return remote(SUM_UP + way, unit, sum_send.at[way, unit], sum_recv.at[way, unit], (up, down)[way])

    def tail_pair_copy(unit):
        at = tail_slot(unit)
        return remote(PAIR_OWN, unit, tail_pair_send.at[at], tail_pair_recv.at[at], pair)

    def tail_relay_copy(way, unit):
        at = tail_slot(unit)
        return remote(
            RELAY_UP + way, unit, tail_relay_send.at[way, at], tail_relay_recv.at[way, at], (up, down)[way]
        )

    def tail_sum_copy(way, unit):
        at = tail_slot(unit)
        return remote(SUM_UP + way, unit, tail_sum_send.at[way, at], tail_sum_recv.at[way, at], (up, down)[way])

    def own_copy(unit):
        return pltpu.make_async_copy(wave_ref.at[unit % 2, unit // 2], own.at[unit], own_sem.at[unit])

    def out_copy(unit):
        return pltpu.make_async_copy(out_buf.at[unit], out_ref.at[unit % 2, unit // 2], out_sem.at[unit])

    def left_copy(slot):
        at = slot % ENV_RING
        return pltpu.make_async_copy(left_ref.at[:, slot], left_buf.at[at], left_sem.at[at])

    def right_copy(slot):
        at = slot % ENV_RING
        return pltpu.make_async_copy(right_ref.at[:, slot], right_buf.at[at], right_sem.at[at])

    barrier = pltpu.get_barrier_semaphore()
    for mate in (up, down, pair, chip_mate, side_mate):
        pl.semaphore_signal(barrier, inc=1, device_id=mate, device_id_type=MESH)

    def start_local(slot, carry):
        own_copy(2 * slot).start()
        own_copy(2 * slot + 1).start()
        left_copy(slot).start()
        right_copy(slot).start()
        return carry

    lax.fori_loop(0, ENV_RING - 1, start_local, 0)
    pl.semaphore_wait(barrier, 5)

    def by_kind(unit, quarters, whole, halves):
        is_quarter, is_whole = one_of(unit, BY_QUARTER), one_of(unit, WHOLE)
        inside = (unit >= 0) & (unit < units)
        pl.when(is_quarter)(quarters)
        if whole is not None:
            pl.when(is_whole)(whole)
        if halves is not None:
            pl.when(inside & jnp.logical_not(is_quarter | is_whole))(halves)

    def start_remote(unit, carry):
        by_kind(
            unit,
            lambda: side_copy(unit, z * quarter, quarter).start(),
            lambda: side_copy(unit, 0, block).start(),
            lambda: side_copy(unit, direct, half).start(),
        )
        chip_copy(unit).start()
        return carry

    lax.fori_loop(0, units, start_remote, 0)

    def stage_quarter(unit):
        side_copy(unit, z * quarter, quarter).wait_recv()
        quarter_up(unit, z).start()
        quarter_down(unit, z).start()

    def stage_hop(unit):
        quarter_up(unit, below).wait_recv()
        hop_up(unit, below).start()
        quarter_down(unit, above).wait_recv()
        hop_down(unit, above).start()

    def stage_half(unit):
        side_copy(unit, direct, half).wait_recv()
        half_up(unit, direct).start()
        half_down(unit, direct).start()

    def write(unit, value):
        limit = dims_ref[unit // 2]
        rows = mpo * slab + lax.broadcasted_iota(jnp.int32, value.shape, 0)
        cols = lax.broadcasted_iota(jnp.int32, value.shape, 1)
        inside = (rows < limit) & (cols < limit)
        out_buf[unit] = jnp.where(inside, value, jnp.zeros_like(value)).astype(bf16)
        out_copy(unit).start()

    top, bottom = pl.ds(0, slab // 2), pl.ds(slab // 2, slab // 2)

    def summed(unit, layer, rows=slice(None)):
        return total[unit % RING, layer, rows] + pair_recv[unit, layer, rows].astype(f32)

    def stage_finish(unit):
        pair_copy(PAIR_OWN, unit).wait_recv()
        sum_copy(0, unit).wait_recv()
        sum_copy(1, unit).wait_recv()
        value = summed(unit, z) + sum_recv[0, unit].astype(f32)
        write(unit, value + sum_recv[1, unit].astype(f32))

    def stage_sum(unit):
        pair_copy(PAIR_ABOVE, unit).wait_recv()
        relay_copy(0, unit).wait_recv()
        sum_send[0, unit, top] = (summed(unit, above, top) + relay_recv[0, unit].astype(f32)).astype(bf16)
        sum_send[0, unit, bottom] = summed(unit, above, bottom).astype(bf16)
        sum_copy(0, unit).start()
        pair_copy(PAIR_BELOW, unit).wait_recv()
        relay_copy(1, unit).wait_recv()
        sum_send[1, unit, top] = summed(unit, below, top).astype(bf16)
        sum_send[1, unit, bottom] = (summed(unit, below, bottom) + relay_recv[1, unit].astype(f32)).astype(bf16)
        sum_copy(1, unit).start()

    def stage_pair(unit):
        pair_copy(PAIR_FAR, unit).wait_recv()
        relay_send[0, unit] = summed(unit, far, top).astype(bf16)
        relay_copy(0, unit).start()
        relay_send[1, unit] = summed(unit, far, bottom).astype(bf16)
        relay_copy(1, unit).start()

    def tail_finish(unit):
        at = tail_slot(unit)
        tail_pair_copy(unit).wait_recv()
        write(unit, tail_total[at, 1, z] + tail_pair_recv[at].astype(f32))

    def tail_pair(unit):
        at = tail_slot(unit)
        tail_sum_copy(0, unit).wait_recv()
        tail_sum_copy(1, unit).wait_recv()
        for side_of in range(2):
            value = tail_total[at, side_of, z] + tail_sum_recv[0, at, side_of].astype(f32)
            value = value + tail_sum_recv[1, at, side_of].astype(f32)
            if side_of == 0:
                tail_pair_send[at] = value.astype(bf16)
                tail_pair_copy(unit).start()
            else:
                tail_total[at, 1, z] = value

    def tail_sum(unit):
        at = tail_slot(unit)
        tail_relay_copy(0, unit).wait_recv()
        tail_sum_send[0, at, 0] = (tail_total[at, 0, above] + tail_relay_recv[0, at].astype(f32)).astype(bf16)
        tail_sum_send[0, at, 1] = tail_total[at, 1, above].astype(bf16)
        tail_sum_copy(0, unit).start()
        tail_relay_copy(1, unit).wait_recv()
        tail_sum_send[1, at, 0] = tail_total[at, 0, below].astype(bf16)
        tail_sum_send[1, at, 1] = (tail_total[at, 1, below] + tail_relay_recv[1, at].astype(f32)).astype(bf16)
        tail_sum_copy(1, unit).start()

    def stage_compute(unit):
        slot = unit // 2
        at = slot % ENV_RING
        own_copy(unit).wait()

        @pl.when(unit % 2 == 0)
        def _():
            left_copy(slot).wait()
            right_copy(slot).wait()

        chip_copy(unit).wait_recv()

        def wait_hops():
            hop_up(unit, far).wait_recv()
            hop_down(unit, far).wait_recv()

        def wait_halves():
            half_up(unit, indirect).wait_recv()
            half_down(unit, indirect).wait_recv()

        by_kind(unit, wait_hops, lambda: side_copy(unit, 0, block).wait_recv(), wait_halves)

        missing = first * ((slots - 1 - slot) // (slots - 1)) + last * (slot // (slots - 1))
        for w in range(2):
            turn = shift_ref[w] * (1 - 2 * core)
            use_side = (turn == 1).astype(f32) * (1 - missing).astype(f32)
            use_chip = (turn == -1).astype(f32)
            use_own = (turn == 0).astype(f32)
            chosen[w] = (
                own[unit] * use_own.astype(bf16)
                + chip[unit] * use_chip.astype(bf16)
                + side[unit] * use_side.astype(bf16)
            )
            theirs = left_buf[at, w, :, 1 - x_lo].reshape(half, block)
            mine = left_buf[at, w, :, x_lo].reshape(half, block)
            rows = jnp.concatenate([theirs, mine], axis=0)
            parts[w] = jnp.dot(rows, chosen[w], preferred_element_type=f32).astype(bf16)
        both = jnp.dot(parts[0], right_buf[at, 0], preferred_element_type=f32) + jnp.dot(
            parts[1], right_buf[at, 1], preferred_element_type=f32
        )

        @pl.when(jnp.logical_not(is_tail(unit)))
        def _():
            pair_send[unit] = both[:half].astype(bf16).reshape(4, slab, block)
            for kind in (PAIR_FAR, PAIR_ABOVE, PAIR_BELOW, PAIR_OWN):
                pair_copy(kind, unit).start()
            total[unit % RING] = both[half:].reshape(4, slab, block)

        @pl.when(is_tail(unit))
        def _():
            tail = tail_slot(unit)
            tail_total[tail] = both.reshape(2, 4, slab, block)
            for way in range(2):
                tail_relay_send[way, tail] = tail_total[tail, way, far].astype(bf16)
                tail_relay_copy(way, unit).start()

    def step(i, carry):
        now = i - AHEAD
        by_kind(i, lambda: stage_quarter(i), None, lambda: stage_half(i))
        ahead = now // 2 + ENV_RING - 1

        @pl.when((now >= 0) & (now % 2 == 0) & (ahead < slots))
        def _():
            start_local(ahead, 0)

        def later(lag, tail, stage):
            unit = now - lag
            kind = is_tail(unit) if tail else jnp.logical_not(is_tail(unit))

            @pl.when((unit >= 0) & (unit < units) & kind)
            def _():
                stage(unit)

        stages = list(zip(LAGS, (False,) * 3, (stage_pair, stage_sum, stage_finish)))
        stages += zip(TAIL_LAGS, (True,) * 3, (tail_sum, tail_pair, tail_finish))
        for lag, tail, stage in sorted(stages, key=lambda item: -item[0]):
            later(lag, tail, stage)

        by_kind(now + 1, lambda: stage_hop(now + 1), None, None)

        @pl.when((now >= 0) & (now < units))
        def _():
            stage_compute(now)

        return carry

    lax.fori_loop(0, AHEAD + units + max(max(LAGS), max(TAIL_LAGS)), step, 0)

    def drain_quarters(unit):
        side_copy(unit, z * quarter, quarter).wait_send()
        quarter_up(unit, z).wait_send()
        quarter_down(unit, z).wait_send()
        hop_up(unit, below).wait_send()
        hop_down(unit, above).wait_send()

    def drain_halves(unit):
        side_copy(unit, direct, half).wait_send()
        half_up(unit, direct).wait_send()
        half_down(unit, direct).wait_send()

    def drain(unit, carry):
        by_kind(
            unit,
            lambda: drain_quarters(unit),
            lambda: side_copy(unit, 0, block).wait_send(),
            lambda: drain_halves(unit),
        )
        out_copy(unit).wait()
        chip_copy(unit).wait_send()

        @pl.when(jnp.logical_not(is_tail(unit)))
        def _():
            for kind in (PAIR_FAR, PAIR_ABOVE, PAIR_BELOW, PAIR_OWN):
                pair_copy(kind, unit).wait_send()
            for way in range(2):
                relay_copy(way, unit).wait_send()
                sum_copy(way, unit).wait_send()

        @pl.when(is_tail(unit))
        def _():
            tail_pair_copy(unit).wait_send()
            for way in range(2):
                tail_relay_copy(way, unit).wait_send()
                tail_sum_copy(way, unit).wait_send()

        return carry

    lax.fori_loop(0, units, drain, 0)


def body(wavefunction, left_env, right_env, block_dims, mpo_shift):
    vectors, slots, block, _ = wavefunction.shape
    slab, units = block // 8, 2 * slots
    left_env = left_env.reshape(2, slots, 4, 2, slab, block)
    bf16, f32 = jnp.bfloat16, jnp.float32
    smem = pl.BlockSpec(memory_space=pltpu.SMEM)
    anywhere = pl.BlockSpec(memory_space=pl.ANY)
    return pl.pallas_call(
        kernel,
        out_shape=jax.ShapeDtypeStruct((vectors, slots, slab, block), bf16),
        in_specs=[smem, smem, anywhere, anywhere, anywhere],
        out_specs=anywhere,
        scratch_shapes=[
            pltpu.VMEM((units, block, block), bf16),
            pltpu.VMEM((units, block, block), bf16),
            pltpu.VMEM((units, block, block), bf16),
            pltpu.VMEM((ENV_RING, 2, 4, 2, slab, block), bf16),
            pltpu.VMEM((ENV_RING, 2, block, block), bf16),
            pltpu.VMEM((2, block, block), bf16),
            pltpu.VMEM((2, block, block), bf16),
            pltpu.VMEM((units, 4, slab, block), bf16),
            pltpu.VMEM((units, 4, slab, block), bf16),
            pltpu.VMEM((RING, 4, slab, block), f32),
            pltpu.VMEM((2, units, slab // 2, block), bf16),
            pltpu.VMEM((2, units, slab // 2, block), bf16),
            pltpu.VMEM((2, units, slab, block), bf16),
            pltpu.VMEM((2, units, slab, block), bf16),
            pltpu.VMEM((Z_SLOTS, 2, 4, slab, block), f32),
            pltpu.VMEM((2, Z_SLOTS, slab, block), bf16),
            pltpu.VMEM((2, Z_SLOTS, slab, block), bf16),
            pltpu.VMEM((2, Z_SLOTS, 2, slab, block), bf16),
            pltpu.VMEM((2, Z_SLOTS, 2, slab, block), bf16),
            pltpu.VMEM((Z_SLOTS, slab, block), bf16),
            pltpu.VMEM((Z_SLOTS, slab, block), bf16),
            pltpu.VMEM((units, slab, block), bf16),
            pltpu.SemaphoreType.DMA((KINDS, units)),
            pltpu.SemaphoreType.DMA((KINDS, units)),
            pltpu.SemaphoreType.DMA((units,)),
            pltpu.SemaphoreType.DMA((ENV_RING,)),
            pltpu.SemaphoreType.DMA((ENV_RING,)),
            pltpu.SemaphoreType.DMA((units,)),
        ],
        compiler_params=pltpu.CompilerParams(
            collective_id=0, has_side_effects=True, vmem_limit_bytes=66 * 1000 * 1000
        ),
        name="matvec",
    )(mpo_shift, block_dims, wavefunction, left_env, right_env)


def solution(mesh):
    placed = (
        P(None, "sec", None, None),
        P("mpo", "sec", None, None),
        P("mpo", "sec", None, None),
        P("sec"),
        P("mpo"),
    )
    return jax.shard_map(
        body, mesh=mesh, in_specs=placed, out_specs=P(None, "sec", "mpo", None), check_vma=False
    )
```

```python
import functools

import jax
import jax.numpy as jnp
from jax import lax
from jax.experimental import pallas as pl
from jax.experimental.pallas import tpu as pltpu
from jax.sharding import PartitionSpec as P

MESH = pl.DeviceIdType.MESH
LAGS = (2, 3, 5)
TAIL_LAGS = (2, 4, 6)
AHEAD = 2
DRAIN_LAG = max(LAGS + TAIL_LAGS) + 1
RING = max(LAGS) + 1
ENV_RING = 4
BY_QUARTER = (0, 1, 2, 3, 5, 6, 11, 12)
WHOLE = (13, 14, 15)
Z_FIRST = (10, 13, 14)
Z_SLOTS = len(Z_FIRST)
CHIP, SIDE, FWD_UP, FWD_DOWN, HOP_UP, HOP_DOWN, RELAY_UP, RELAY_DOWN, SUM_UP, SUM_DOWN = range(10)
PAIR_FAR, PAIR_ABOVE, PAIR_BELOW, PAIR_OWN = range(10, 14)
KINDS = 14


def one_of(unit, members):
    found = unit == members[0]
    for member in members[1:]:
        found = found | (unit == member)
    return found


def is_tail(unit):
    return one_of(unit, Z_FIRST)


def tail_slot(unit):
    return sum((unit > member).astype(jnp.int32) for member in Z_FIRST[:-1])


def kernel(
    shift_ref, dims_ref, wave_ref, left_ref, right_ref, out_ref,
    own, chip, side, left_buf, right_buf, chosen, parts,
    pair_send, pair_recv, total, relay_send, relay_recv, sum_send, sum_recv,
    tail_total, tail_relay_send, tail_relay_recv, tail_sum_send, tail_sum_recv, tail_pair_send, tail_pair_recv,
    out_buf, send_sem, recv_sem, own_sem, left_sem, right_sem, out_sem,
):
    bf16, f32 = jnp.bfloat16, jnp.float32
    slots, block = wave_ref.shape[1], wave_ref.shape[2]
    units = 2 * slots
    half, quarter, eighth = block // 2, block // 4, block // 8
    slab = block // 8
    mpo = lax.axis_index("mpo")
    sec = lax.axis_index("sec")
    secs = lax.axis_size("sec")
    core = sec % 2
    z = mpo // 2
    x_lo = mpo % 2
    above, below, far = (z + 1) % 4, (z + 3) % 4, (z + 2) % 4
    direct = (z % 2) * half
    indirect = half - direct
    up = ((mpo + 2) % 8, sec)
    down = ((mpo + 6) % 8, sec)
    pair = (mpo + 1 - 2 * x_lo, sec)
    chip_mate = (mpo, sec + 1 - 2 * core)
    side_mate = (mpo + 1 - 2 * x_lo, (sec + secs - 1 + 2 * core) % secs)
    first = (secs - 1 - sec) // (secs - 1)
    last = sec // (secs - 1)

    def remote(kind, unit, src, dst, device):
        return pltpu.make_async_remote_copy(
            src_ref=src, dst_ref=dst, send_sem=send_sem.at[kind, unit],
            recv_sem=recv_sem.at[kind, unit], device_id=device, device_id_type=MESH,
        )

    def chip_copy(unit):
        return remote(CHIP, unit, wave_ref.at[unit % 2, unit // 2], chip.at[unit], chip_mate)

    def side_copy(unit, start, size):
        source = (unit // 2 + first - last + slots) % slots
        rows = pl.ds(start, size)
        return remote(SIDE, unit, wave_ref.at[unit % 2, source, rows], side.at[unit, rows], side_mate)

    def pass_on(kind, unit, start, size, device):
        piece = side.at[unit, pl.ds(start, size)]
        return remote(kind, unit, piece, piece, device)

    def half_up(unit, start):
        return pass_on(FWD_UP, unit, start, quarter, up)

    def half_down(unit, start):
        return pass_on(FWD_DOWN, unit, start + quarter, quarter, down)

    def quarter_up(unit, layer):
        return pass_on(FWD_UP, unit, layer * quarter, quarter, up)

    def quarter_down(unit, layer):
        return pass_on(FWD_DOWN, unit, layer * quarter, quarter, down)

    def hop_up(unit, layer):
        return pass_on(HOP_UP, unit, layer * quarter, eighth, up)

    def hop_down(unit, layer):
        return pass_on(HOP_DOWN, unit, layer * quarter + eighth, eighth, down)

    def pair_copy(kind, unit):
        layer = {PAIR_FAR: far, PAIR_ABOVE: above, PAIR_BELOW: below, PAIR_OWN: z}[kind]
        return remote(kind, unit, pair_send.at[unit, layer], pair_recv.at[unit, layer], pair)

    def relay_copy(way, unit):
        return remote(RELAY_UP + way, unit, relay_send.at[way, unit], relay_recv.at[way, unit], (up, down)[way])

    def sum_copy(way, unit):
        return remote(SUM_UP + way, unit, sum_send.at[way, unit], sum_recv.at[way, unit], (up, down)[way])

    def tail_pair_copy(unit):
        at = tail_slot(unit)
        return remote(PAIR_OWN, unit, tail_pair_send.at[at], tail_pair_recv.at[at], pair)

    def tail_relay_copy(way, unit):
        at = tail_slot(unit)
        return remote(
            RELAY_UP + way, unit, tail_relay_send.at[way, at], tail_relay_recv.at[way, at], (up, down)[way]
        )

    def tail_sum_copy(way, unit):
        at = tail_slot(unit)
        return remote(SUM_UP + way, unit, tail_sum_send.at[way, at], tail_sum_recv.at[way, at], (up, down)[way])

    def own_copy(unit):
        return pltpu.make_async_copy(wave_ref.at[unit % 2, unit // 2], own.at[unit], own_sem.at[unit])

    def out_copy(unit):
        return pltpu.make_async_copy(out_buf.at[unit], out_ref.at[unit % 2, unit // 2], out_sem.at[unit])

    def left_copy(slot):
        at = slot % ENV_RING
        return pltpu.make_async_copy(left_ref.at[:, slot], left_buf.at[at], left_sem.at[at])

    def right_copy(slot):
        at = slot % ENV_RING
        return pltpu.make_async_copy(right_ref.at[:, slot], right_buf.at[at], right_sem.at[at])

    barrier = pltpu.get_barrier_semaphore()
    for mate in (up, down, pair, chip_mate, side_mate):
        pl.semaphore_signal(barrier, inc=1, device_id=mate, device_id_type=MESH)

    def start_local(slot, carry):
        own_copy(2 * slot).start()
        own_copy(2 * slot + 1).start()
        left_copy(slot).start()
        right_copy(slot).start()
        return carry

    lax.fori_loop(0, ENV_RING - 1, start_local, 0)
    pl.semaphore_wait(barrier, 5)

    def by_kind(unit, quarters, whole, halves):
        is_quarter, is_whole = one_of(unit, BY_QUARTER), one_of(unit, WHOLE)
        inside = (unit >= 0) & (unit < units)
        pl.when(is_quarter)(quarters)
        if whole is not None:
            pl.when(is_whole)(whole)
        if halves is not None:
            pl.when(inside & jnp.logical_not(is_quarter | is_whole))(halves)

    def start_remote(unit, carry):
        by_kind(
            unit,
            lambda: side_copy(unit, z * quarter, quarter).start(),
            lambda: side_copy(unit, 0, block).start(),
            lambda: side_copy(unit, direct, half).start(),
        )
        chip_copy(unit).start()
        return carry

    lax.fori_loop(0, units, start_remote, 0)

    def stage_quarter(unit):
        side_copy(unit, z * quarter, quarter).wait_recv()
        quarter_up(unit, z).start()
        quarter_down(unit, z).start()

    def stage_hop(unit):
        quarter_up(unit, below).wait_recv()
        hop_up(unit, below).start()
        quarter_down(unit, above).wait_recv()
        hop_down(unit, above).start()

    def stage_half(unit):
        side_copy(unit, direct, half).wait_recv()
        half_up(unit, direct).start()
        half_down(unit, direct).start()

    def write(unit, value):
        limit = dims_ref[unit // 2]
        rows = mpo * slab + lax.broadcasted_iota(jnp.int32, value.shape, 0)
        cols = lax.broadcasted_iota(jnp.int32, value.shape, 1)
        inside = (rows < limit) & (cols < limit)
        out_buf[unit] = jnp.where(inside, value, jnp.zeros_like(value)).astype(bf16)
        out_copy(unit).start()

    top, bottom = pl.ds(0, slab // 2), pl.ds(slab // 2, slab // 2)

    def summed(unit, layer, rows=slice(None)):
        return total[unit % RING, layer, rows] + pair_recv[unit, layer, rows].astype(f32)

    def stage_finish(unit):
        pair_copy(PAIR_OWN, unit).wait_recv()
        sum_copy(0, unit).wait_recv()
        sum_copy(1, unit).wait_recv()
        value = summed(unit, z) + sum_recv[0, unit].astype(f32)
        write(unit, value + sum_recv[1, unit].astype(f32))

    def stage_sum(unit):
        pair_copy(PAIR_ABOVE, unit).wait_recv()
        relay_copy(0, unit).wait_recv()
        sum_send[0, unit, top] = (summed(unit, above, top) + relay_recv[0, unit].astype(f32)).astype(bf16)
        sum_send[0, unit, bottom] = summed(unit, above, bottom).astype(bf16)
        sum_copy(0, unit).start()
        pair_copy(PAIR_BELOW, unit).wait_recv()
        relay_copy(1, unit).wait_recv()
        sum_send[1, unit, top] = summed(unit, below, top).astype(bf16)
        sum_send[1, unit, bottom] = (summed(unit, below, bottom) + relay_recv[1, unit].astype(f32)).astype(bf16)
        sum_copy(1, unit).start()

    def stage_pair(unit):
        pair_copy(PAIR_FAR, unit).wait_recv()
        relay_send[0, unit] = summed(unit, far, top).astype(bf16)
        relay_copy(0, unit).start()
        relay_send[1, unit] = summed(unit, far, bottom).astype(bf16)
        relay_copy(1, unit).start()

    def tail_finish(unit):
        at = tail_slot(unit)
        tail_pair_copy(unit).wait_recv()
        write(unit, tail_total[at, 1, z] + tail_pair_recv[at].astype(f32))

    def tail_pair(unit):
        at = tail_slot(unit)
        tail_sum_copy(0, unit).wait_recv()
        tail_sum_copy(1, unit).wait_recv()
        for side_of in range(2):
            value = tail_total[at, side_of, z] + tail_sum_recv[0, at, side_of].astype(f32)
            value = value + tail_sum_recv[1, at, side_of].astype(f32)
            if side_of == 0:
                tail_pair_send[at] = value.astype(bf16)
                tail_pair_copy(unit).start()
            else:
                tail_total[at, 1, z] = value

    def tail_sum(unit):
        at = tail_slot(unit)
        tail_relay_copy(0, unit).wait_recv()
        tail_sum_send[0, at, 0] = (tail_total[at, 0, above] + tail_relay_recv[0, at].astype(f32)).astype(bf16)
        tail_sum_send[0, at, 1] = tail_total[at, 1, above].astype(bf16)
        tail_sum_copy(0, unit).start()
        tail_relay_copy(1, unit).wait_recv()
        tail_sum_send[1, at, 0] = tail_total[at, 0, below].astype(bf16)
        tail_sum_send[1, at, 1] = (tail_total[at, 1, below] + tail_relay_recv[1, at].astype(f32)).astype(bf16)
        tail_sum_copy(1, unit).start()

    def stage_compute(unit):
        slot = unit // 2
        at = slot % ENV_RING
        own_copy(unit).wait()

        @pl.when(unit % 2 == 0)
        def _():
            left_copy(slot).wait()
            right_copy(slot).wait()

        chip_copy(unit).wait_recv()

        def wait_hops():
            hop_up(unit, far).wait_recv()
            hop_down(unit, far).wait_recv()

        def wait_halves():
            half_up(unit, indirect).wait_recv()
            half_down(unit, indirect).wait_recv()

        by_kind(unit, wait_hops, lambda: side_copy(unit, 0, block).wait_recv(), wait_halves)

        missing = first * ((slots - 1 - slot) // (slots - 1)) + last * (slot // (slots - 1))
        for w in range(2):
            turn = shift_ref[w] * (1 - 2 * core)
            use_side = (turn == 1).astype(f32) * (1 - missing).astype(f32)
            use_chip = (turn == -1).astype(f32)
            use_own = (turn == 0).astype(f32)
            chosen[w] = (
                own[unit] * use_own.astype(bf16)
                + chip[unit] * use_chip.astype(bf16)
                + side[unit] * use_side.astype(bf16)
            )
            theirs = left_buf[at, w, :, 1 - x_lo].reshape(half, block)
            mine = left_buf[at, w, :, x_lo].reshape(half, block)
            rows = jnp.concatenate([theirs, mine], axis=0)
            parts[w] = jnp.dot(rows, chosen[w], preferred_element_type=f32).astype(bf16)
        both = jnp.dot(parts[0], right_buf[at, 0], preferred_element_type=f32) + jnp.dot(
            parts[1], right_buf[at, 1], preferred_element_type=f32
        )

        @pl.when(jnp.logical_not(is_tail(unit)))
        def _():
            pair_send[unit] = both[:half].astype(bf16).reshape(4, slab, block)
            for kind in (PAIR_FAR, PAIR_ABOVE, PAIR_BELOW, PAIR_OWN):
                pair_copy(kind, unit).start()
            total[unit % RING] = both[half:].reshape(4, slab, block)

        @pl.when(is_tail(unit))
        def _():
            tail = tail_slot(unit)
            tail_total[tail] = both.reshape(2, 4, slab, block)
            for way in range(2):
                tail_relay_send[way, tail] = tail_total[tail, way, far].astype(bf16)
                tail_relay_copy(way, unit).start()

    def drain_quarters(unit):
        side_copy(unit, z * quarter, quarter).wait_send()
        quarter_up(unit, z).wait_send()
        quarter_down(unit, z).wait_send()
        hop_up(unit, below).wait_send()
        hop_down(unit, above).wait_send()

    def drain_halves(unit):
        side_copy(unit, direct, half).wait_send()
        half_up(unit, direct).wait_send()
        half_down(unit, direct).wait_send()

    def drain(unit):
        by_kind(
            unit,
            lambda: drain_quarters(unit),
            lambda: side_copy(unit, 0, block).wait_send(),
            lambda: drain_halves(unit),
        )
        out_copy(unit).wait()
        chip_copy(unit).wait_send()

        @pl.when(jnp.logical_not(is_tail(unit)))
        def _():
            for kind in (PAIR_FAR, PAIR_ABOVE, PAIR_BELOW, PAIR_OWN):
                pair_copy(kind, unit).wait_send()
            for way in range(2):
                relay_copy(way, unit).wait_send()
                sum_copy(way, unit).wait_send()

        @pl.when(is_tail(unit))
        def _():
            tail_pair_copy(unit).wait_send()
            for way in range(2):
                tail_relay_copy(way, unit).wait_send()
                tail_sum_copy(way, unit).wait_send()

    def step(i, carry):
        now = i - AHEAD
        by_kind(i, lambda: stage_quarter(i), None, lambda: stage_half(i))
        ahead = now // 2 + ENV_RING - 1

        @pl.when((now >= 0) & (now % 2 == 0) & (ahead < slots))
        def _():
            start_local(ahead, 0)

        def later(lag, tail, stage):
            unit = now - lag
            kind = is_tail(unit) if tail else jnp.logical_not(is_tail(unit))

            @pl.when((unit >= 0) & (unit < units) & kind)
            def _():
                stage(unit)

        stages = list(zip(LAGS, (False,) * 3, (stage_pair, stage_sum, stage_finish)))
        stages += zip(TAIL_LAGS, (True,) * 3, (tail_sum, tail_pair, tail_finish))
        for lag, tail, stage in sorted(stages, key=lambda item: -item[0]):
            later(lag, tail, stage)

        by_kind(now + 1, lambda: stage_hop(now + 1), None, None)

        @pl.when((now >= 0) & (now < units))
        def _():
            stage_compute(now)

        done = now - DRAIN_LAG

        @pl.when((done >= 0) & (done < units))
        def _():
            drain(done)

        return carry

    lax.fori_loop(0, AHEAD + units + DRAIN_LAG, step, 0)


def body(wavefunction, left_env, right_env, block_dims, mpo_shift):
    vectors, slots, block, _ = wavefunction.shape
    slab, units = block // 8, 2 * slots
    left_env = left_env.reshape(2, slots, 4, 2, slab, block)
    bf16, f32 = jnp.bfloat16, jnp.float32
    smem = pl.BlockSpec(memory_space=pltpu.SMEM)
    anywhere = pl.BlockSpec(memory_space=pl.ANY)
    return pl.pallas_call(
        kernel,
        out_shape=jax.ShapeDtypeStruct((vectors, slots, slab, block), bf16),
        in_specs=[smem, smem, anywhere, anywhere, anywhere],
        out_specs=anywhere,
        scratch_shapes=[
            pltpu.VMEM((units, block, block), bf16),
            pltpu.VMEM((units, block, block), bf16),
            pltpu.VMEM((units, block, block), bf16),
            pltpu.VMEM((ENV_RING, 2, 4, 2, slab, block), bf16),
            pltpu.VMEM((ENV_RING, 2, block, block), bf16),
            pltpu.VMEM((2, block, block), bf16),
            pltpu.VMEM((2, block, block), bf16),
            pltpu.VMEM((units, 4, slab, block), bf16),
            pltpu.VMEM((units, 4, slab, block), bf16),
            pltpu.VMEM((RING, 4, slab, block), f32),
            pltpu.VMEM((2, units, slab // 2, block), bf16),
            pltpu.VMEM((2, units, slab // 2, block), bf16),
            pltpu.VMEM((2, units, slab, block), bf16),
            pltpu.VMEM((2, units, slab, block), bf16),
            pltpu.VMEM((Z_SLOTS, 2, 4, slab, block), f32),
            pltpu.VMEM((2, Z_SLOTS, slab, block), bf16),
            pltpu.VMEM((2, Z_SLOTS, slab, block), bf16),
            pltpu.VMEM((2, Z_SLOTS, 2, slab, block), bf16),
            pltpu.VMEM((2, Z_SLOTS, 2, slab, block), bf16),
            pltpu.VMEM((Z_SLOTS, slab, block), bf16),
            pltpu.VMEM((Z_SLOTS, slab, block), bf16),
            pltpu.VMEM((units, slab, block), bf16),
            pltpu.SemaphoreType.DMA((KINDS, units)),
            pltpu.SemaphoreType.DMA((KINDS, units)),
            pltpu.SemaphoreType.DMA((units,)),
            pltpu.SemaphoreType.DMA((ENV_RING,)),
            pltpu.SemaphoreType.DMA((ENV_RING,)),
            pltpu.SemaphoreType.DMA((units,)),
        ],
        compiler_params=pltpu.CompilerParams(
            collective_id=0, has_side_effects=True, vmem_limit_bytes=66 * 1000 * 1000
        ),
        name="matvec",
    )(mpo_shift, block_dims, wavefunction, left_env, right_env)


def solution(mesh):
    placed = (
        P(None, "sec", None, None),
        P("mpo", "sec", None, None),
        P("mpo", "sec", None, None),
        P("sec"),
        P("mpo"),
    )
    return jax.shard_map(
        body, mesh=mesh, in_specs=placed, out_specs=P(None, "sec", "mpo", None), check_vma=False
    )
```

```python
import functools

import jax
import jax.numpy as jnp
from jax import lax
from jax.experimental import pallas as pl
from jax.experimental.pallas import tpu as pltpu
from jax.sharding import PartitionSpec as P

MESH = pl.DeviceIdType.MESH
LAGS = (2, 4, 6)
TAIL_LAGS = (2, 4, 6)
AHEAD = 2
DRAIN_LAG = max(LAGS + TAIL_LAGS) + 1
RING = max(LAGS) + 1
ENV_RING = 3
BY_QUARTER = (3, 4, 10, 13)
THROUGH_PAIR = (0, 1, 2, 5, 6)
WHOLE = (12, 14, 15)
Z_FIRST = (2, 8, 11, 14)
Z_SLOTS = len(Z_FIRST)
CHIP, SIDE, FWD_UP, FWD_DOWN, HOP_UP, HOP_DOWN, RELAY_UP, RELAY_DOWN, SUM_UP, SUM_DOWN = range(10)
PAIR_FAR, PAIR_ABOVE, PAIR_BELOW, PAIR_OWN, FWD_PAIR = range(10, 15)
KINDS = 15


def one_of(unit, members):
    found = unit == members[0]
    for member in members[1:]:
        found = found | (unit == member)
    return found


def is_tail(unit):
    return one_of(unit, Z_FIRST)


def tail_slot(unit):
    return sum((unit > member).astype(jnp.int32) for member in Z_FIRST[:-1])


def kernel(
    shift_ref, dims_ref, wave_ref, left_ref, right_ref, out_ref,
    own, chip, side, left_buf, right_buf, chosen, parts,
    pair_send, pair_recv, total, relay_send, relay_recv, sum_send, sum_recv,
    tail_total, tail_relay_send, tail_relay_recv, tail_sum_send, tail_sum_recv, tail_pair_send, tail_pair_recv,
    out_buf, send_sem, recv_sem, own_sem, left_sem, right_sem, out_sem,
):
    bf16, f32 = jnp.bfloat16, jnp.float32
    slots, block = wave_ref.shape[1], wave_ref.shape[2]
    units = 2 * slots
    half, quarter, eighth = block // 2, block // 4, block // 8
    slab = block // 8
    mpo = lax.axis_index("mpo")
    sec = lax.axis_index("sec")
    secs = lax.axis_size("sec")
    core = sec % 2
    z = mpo // 2
    x_lo = mpo % 2
    above, below, far = (z + 1) % 4, (z + 3) % 4, (z + 2) % 4
    direct = (z % 2) * half
    indirect = half - direct
    near_mine, near_theirs = direct + x_lo * quarter, direct + (1 - x_lo) * quarter
    off_mine, off_theirs = indirect + x_lo * quarter, indirect + (1 - x_lo) * quarter
    up = ((mpo + 2) % 8, sec)
    down = ((mpo + 6) % 8, sec)
    pair = (mpo + 1 - 2 * x_lo, sec)
    chip_mate = (mpo, sec + 1 - 2 * core)
    side_mate = (mpo + 1 - 2 * x_lo, (sec + secs - 1 + 2 * core) % secs)
    first = (secs - 1 - sec) // (secs - 1)
    last = sec // (secs - 1)

    def remote(kind, unit, src, dst, device):
        return pltpu.make_async_remote_copy(
            src_ref=src, dst_ref=dst, send_sem=send_sem.at[kind, unit],
            recv_sem=recv_sem.at[kind, unit], device_id=device, device_id_type=MESH,
        )

    def chip_copy(unit):
        return remote(CHIP, unit, wave_ref.at[unit % 2, unit // 2], chip.at[unit], chip_mate)

    def side_copy(unit, start, size):
        source = (unit // 2 + first - last + slots) % slots
        rows = pl.ds(start, size)
        return remote(SIDE, unit, wave_ref.at[unit % 2, source, rows], side.at[unit, rows], side_mate)

    def pass_on(kind, unit, start, size, device):
        piece = side.at[unit, pl.ds(start, size)]
        return remote(kind, unit, piece, piece, device)

    def half_up(unit, start):
        return pass_on(FWD_UP, unit, start, quarter, up)

    def half_down(unit, start):
        return pass_on(FWD_DOWN, unit, start + quarter, quarter, down)

    def quarter_up(unit, layer):
        return pass_on(FWD_UP, unit, layer * quarter, quarter, up)

    def quarter_down(unit, layer):
        return pass_on(FWD_DOWN, unit, layer * quarter, quarter, down)

    def hop_up(unit, layer):
        return pass_on(HOP_UP, unit, layer * quarter, eighth, up)

    def hop_down(unit, layer):
        return pass_on(HOP_DOWN, unit, layer * quarter + eighth, eighth, down)

    def pair_copy(kind, unit):
        layer = {PAIR_FAR: far, PAIR_ABOVE: above, PAIR_BELOW: below, PAIR_OWN: z}[kind]
        return remote(kind, unit, pair_send.at[unit, layer], pair_recv.at[unit, layer], pair)

    def relay_copy(way, unit):
        return remote(RELAY_UP + way, unit, relay_send.at[way, unit], relay_recv.at[way, unit], (up, down)[way])

    def sum_copy(way, unit):
        return remote(SUM_UP + way, unit, sum_send.at[way, unit], sum_recv.at[way, unit], (up, down)[way])

    def tail_pair_copy(unit):
        at = tail_slot(unit)
        return remote(PAIR_OWN, unit, tail_pair_send.at[at], tail_pair_recv.at[at], pair)

    def tail_relay_copy(way, unit):
        at = tail_slot(unit)
        return remote(
            RELAY_UP + way, unit, tail_relay_send.at[way, at], tail_relay_recv.at[way, at], (up, down)[way]
        )

    def tail_sum_copy(way, unit):
        at = tail_slot(unit)
        return remote(SUM_UP + way, unit, tail_sum_send.at[way, at], tail_sum_recv.at[way, at], (up, down)[way])

    def own_copy(unit):
        return pltpu.make_async_copy(wave_ref.at[unit % 2, unit // 2], own.at[unit], own_sem.at[unit])

    def out_copy(unit):
        return pltpu.make_async_copy(out_buf.at[unit], out_ref.at[unit % 2, unit // 2], out_sem.at[unit])

    def left_copy(slot):
        at = slot % ENV_RING
        return pltpu.make_async_copy(left_ref.at[:, slot], left_buf.at[at], left_sem.at[at])

    def right_copy(slot):
        at = slot % ENV_RING
        return pltpu.make_async_copy(right_ref.at[:, slot], right_buf.at[at], right_sem.at[at])

    barrier = pltpu.get_barrier_semaphore()
    for mate in (up, down, pair, chip_mate, side_mate):
        pl.semaphore_signal(barrier, inc=1, device_id=mate, device_id_type=MESH)

    def start_local(slot, carry):
        own_copy(2 * slot).start()
        own_copy(2 * slot + 1).start()
        left_copy(slot).start()
        right_copy(slot).start()
        return carry

    lax.fori_loop(0, ENV_RING - 1, start_local, 0)
    pl.semaphore_wait(barrier, 5)

    def by_kind(unit, quarters=None, through=None, whole=None, halves=None):
        kinds = [one_of(unit, members) for members in (BY_QUARTER, THROUGH_PAIR, WHOLE)]
        kinds.append((unit >= 0) & (unit < units) & jnp.logical_not(kinds[0] | kinds[1] | kinds[2]))
        for found, action in zip(kinds, (quarters, through, whole, halves)):
            if action is not None:
                pl.when(found)(action)

    def start_remote(unit, carry):
        by_kind(
            unit,
            lambda: side_copy(unit, z * quarter, quarter).start(),
            lambda: side_copy(unit, near_theirs, quarter).start(),
            lambda: side_copy(unit, 0, block).start(),
            lambda: side_copy(unit, direct, half).start(),
        )
        chip_copy(unit).start()
        return carry

    lax.fori_loop(0, units, start_remote, 0)

    def stage_quarter(unit):
        side_copy(unit, z * quarter, quarter).wait_recv()
        quarter_up(unit, z).start()
        quarter_down(unit, z).start()

    def stage_hop(unit):
        quarter_up(unit, below).wait_recv()
        hop_up(unit, below).start()
        quarter_down(unit, above).wait_recv()
        hop_down(unit, above).start()

    def through_pair(unit, near):
        return [pass_on(FWD_PAIR, unit, near, quarter, pair)]

    def through_forward(unit, near):
        return [
            pass_on(FWD_UP, unit, near, eighth, up),
            pass_on(FWD_DOWN, unit, near + eighth, eighth, down),
        ]

    def through_hop(unit, off):
        return [
            pass_on(HOP_UP, unit, off, eighth, up),
            pass_on(HOP_DOWN, unit, off + eighth, eighth, down),
        ]

    def stage_through(unit):
        side_copy(unit, near_mine, quarter).wait_recv()
        for copy in through_pair(unit, near_mine) + through_forward(unit, near_mine):
            copy.start()

    def stage_through_hop(unit):
        through_pair(unit, near_theirs)[0].wait_recv()
        for copy in through_hop(unit, near_theirs):
            copy.start()

    def stage_half(unit):
        side_copy(unit, direct, half).wait_recv()
        half_up(unit, direct).start()
        half_down(unit, direct).start()

    def write(unit, value):
        limit = dims_ref[unit // 2]
        rows = mpo * slab + lax.broadcasted_iota(jnp.int32, value.shape, 0)
        cols = lax.broadcasted_iota(jnp.int32, value.shape, 1)
        inside = (rows < limit) & (cols < limit)
        out_buf[unit] = jnp.where(inside, value, jnp.zeros_like(value)).astype(bf16)
        out_copy(unit).start()

    top, bottom = pl.ds(0, slab // 2), pl.ds(slab // 2, slab // 2)

    def summed(unit, layer, rows=slice(None)):
        return total[unit % RING, layer, rows] + pair_recv[unit, layer, rows].astype(f32)

    def stage_finish(unit):
        pair_copy(PAIR_OWN, unit).wait_recv()
        sum_copy(0, unit).wait_recv()
        sum_copy(1, unit).wait_recv()
        value = summed(unit, z) + sum_recv[0, unit].astype(f32)
        write(unit, value + sum_recv[1, unit].astype(f32))

    def stage_sum(unit):
        pair_copy(PAIR_ABOVE, unit).wait_recv()
        relay_copy(0, unit).wait_recv()
        sum_send[0, unit, top] = (summed(unit, above, top) + relay_recv[0, unit].astype(f32)).astype(bf16)
        sum_send[0, unit, bottom] = summed(unit, above, bottom).astype(bf16)
        sum_copy(0, unit).start()
        pair_copy(PAIR_BELOW, unit).wait_recv()
        relay_copy(1, unit).wait_recv()
        sum_send[1, unit, top] = summed(unit, below, top).astype(bf16)
        sum_send[1, unit, bottom] = (summed(unit, below, bottom) + relay_recv[1, unit].astype(f32)).astype(bf16)
        sum_copy(1, unit).start()

    def stage_pair(unit):
        pair_copy(PAIR_FAR, unit).wait_recv()
        relay_send[0, unit] = summed(unit, far, top).astype(bf16)
        relay_copy(0, unit).start()
        relay_send[1, unit] = summed(unit, far, bottom).astype(bf16)
        relay_copy(1, unit).start()

    def tail_finish(unit):
        at = tail_slot(unit)
        tail_pair_copy(unit).wait_recv()
        write(unit, tail_total[at, 1, z] + tail_pair_recv[at].astype(f32))

    def tail_pair(unit):
        at = tail_slot(unit)
        tail_sum_copy(0, unit).wait_recv()
        tail_sum_copy(1, unit).wait_recv()
        for side_of in range(2):
            value = tail_total[at, side_of, z] + tail_sum_recv[0, at, side_of].astype(f32)
            value = value + tail_sum_recv[1, at, side_of].astype(f32)
            if side_of == 0:
                tail_pair_send[at] = value.astype(bf16)
                tail_pair_copy(unit).start()
            else:
                tail_total[at, 1, z] = value

    def tail_sum(unit):
        at = tail_slot(unit)
        tail_relay_copy(0, unit).wait_recv()
        tail_sum_send[0, at, 0] = (tail_total[at, 0, above] + tail_relay_recv[0, at].astype(f32)).astype(bf16)
        tail_sum_send[0, at, 1] = tail_total[at, 1, above].astype(bf16)
        tail_sum_copy(0, unit).start()
        tail_relay_copy(1, unit).wait_recv()
        tail_sum_send[1, at, 0] = tail_total[at, 0, below].astype(bf16)
        tail_sum_send[1, at, 1] = (tail_total[at, 1, below] + tail_relay_recv[1, at].astype(f32)).astype(bf16)
        tail_sum_copy(1, unit).start()

    def stage_compute(unit):
        slot = unit // 2
        at = slot % ENV_RING
        own_copy(unit).wait()

        @pl.when(unit % 2 == 0)
        def _():
            left_copy(slot).wait()
            right_copy(slot).wait()

        chip_copy(unit).wait_recv()

        def wait_hops():
            hop_up(unit, far).wait_recv()
            hop_down(unit, far).wait_recv()

        def wait_halves():
            half_up(unit, indirect).wait_recv()
            half_down(unit, indirect).wait_recv()

        def wait_through():
            for copy in through_forward(unit, off_mine) + through_hop(unit, off_theirs):
                copy.wait_recv()

        by_kind(unit, wait_hops, wait_through, lambda: side_copy(unit, 0, block).wait_recv(), wait_halves)

        missing = first * ((slots - 1 - slot) // (slots - 1)) + last * (slot // (slots - 1))
        for w in range(2):
            turn = shift_ref[w] * (1 - 2 * core)
            use_side = (turn == 1).astype(f32) * (1 - missing).astype(f32)
            use_chip = (turn == -1).astype(f32)
            use_own = (turn == 0).astype(f32)
            chosen[w] = (
                own[unit] * use_own.astype(bf16)
                + chip[unit] * use_chip.astype(bf16)
                + side[unit] * use_side.astype(bf16)
            )
            theirs = left_buf[at, w, :, 1 - x_lo].reshape(half, block)
            mine = left_buf[at, w, :, x_lo].reshape(half, block)
            rows = jnp.concatenate([theirs, mine], axis=0)
            parts[w] = jnp.dot(rows, chosen[w], preferred_element_type=f32).astype(bf16)
        both = jnp.dot(parts[0], right_buf[at, 0], preferred_element_type=f32) + jnp.dot(
            parts[1], right_buf[at, 1], preferred_element_type=f32
        )

        @pl.when(jnp.logical_not(is_tail(unit)))
        def _():
            pair_send[unit] = both[:half].astype(bf16).reshape(4, slab, block)
            for kind in (PAIR_FAR, PAIR_ABOVE, PAIR_BELOW, PAIR_OWN):
                pair_copy(kind, unit).start()
            total[unit % RING] = both[half:].reshape(4, slab, block)

        @pl.when(is_tail(unit))
        def _():
            tail = tail_slot(unit)
            tail_total[tail] = both.reshape(2, 4, slab, block)
            for way in range(2):
                tail_relay_send[way, tail] = tail_total[tail, way, far].astype(bf16)
                tail_relay_copy(way, unit).start()

    def drain_quarters(unit):
        side_copy(unit, z * quarter, quarter).wait_send()
        quarter_up(unit, z).wait_send()
        quarter_down(unit, z).wait_send()
        hop_up(unit, below).wait_send()
        hop_down(unit, above).wait_send()

    def drain_through(unit):
        side_copy(unit, near_theirs, quarter).wait_send()
        copies = through_pair(unit, near_mine) + through_forward(unit, near_mine)
        for copy in copies + through_hop(unit, near_theirs):
            copy.wait_send()

    def drain_halves(unit):
        side_copy(unit, direct, half).wait_send()
        half_up(unit, direct).wait_send()
        half_down(unit, direct).wait_send()

    def drain(unit):
        by_kind(
            unit,
            lambda: drain_quarters(unit),
            lambda: drain_through(unit),
            lambda: side_copy(unit, 0, block).wait_send(),
            lambda: drain_halves(unit),
        )
        out_copy(unit).wait()
        chip_copy(unit).wait_send()

        @pl.when(jnp.logical_not(is_tail(unit)))
        def _():
            for kind in (PAIR_FAR, PAIR_ABOVE, PAIR_BELOW, PAIR_OWN):
                pair_copy(kind, unit).wait_send()
            for way in range(2):
                relay_copy(way, unit).wait_send()
                sum_copy(way, unit).wait_send()

        @pl.when(is_tail(unit))
        def _():
            tail_pair_copy(unit).wait_send()
            for way in range(2):
                tail_relay_copy(way, unit).wait_send()
                tail_sum_copy(way, unit).wait_send()

    def step(i, carry):
        now = i - AHEAD
        by_kind(i, lambda: stage_quarter(i), lambda: stage_through(i), None, lambda: stage_half(i))
        ahead = now // 2 + ENV_RING - 1

        @pl.when((now >= 0) & (now % 2 == 0) & (ahead < slots))
        def _():
            start_local(ahead, 0)

        def later(lag, tail, stage):
            unit = now - lag
            kind = is_tail(unit) if tail else jnp.logical_not(is_tail(unit))

            @pl.when((unit >= 0) & (unit < units) & kind)
            def _():
                stage(unit)

        stages = list(zip(LAGS, (False,) * 3, (stage_pair, stage_sum, stage_finish)))
        stages += zip(TAIL_LAGS, (True,) * 3, (tail_sum, tail_pair, tail_finish))
        for lag, tail, stage in sorted(stages, key=lambda item: -item[0]):
            later(lag, tail, stage)

        by_kind(now + 1, lambda: stage_hop(now + 1), lambda: stage_through_hop(now + 1))

        @pl.when((now >= 0) & (now < units))
        def _():
            stage_compute(now)

        done = now - DRAIN_LAG

        @pl.when((done >= 0) & (done < units))
        def _():
            drain(done)

        return carry

    lax.fori_loop(0, AHEAD + units + DRAIN_LAG, step, 0)


def body(wavefunction, left_env, right_env, block_dims, mpo_shift):
    vectors, slots, block, _ = wavefunction.shape
    slab, units = block // 8, 2 * slots
    left_env = left_env.reshape(2, slots, 4, 2, slab, block)
    bf16, f32 = jnp.bfloat16, jnp.float32
    smem = pl.BlockSpec(memory_space=pltpu.SMEM)
    anywhere = pl.BlockSpec(memory_space=pl.ANY)
    return pl.pallas_call(
        kernel,
        out_shape=jax.ShapeDtypeStruct((vectors, slots, slab, block), bf16),
        in_specs=[smem, smem, anywhere, anywhere, anywhere],
        out_specs=anywhere,
        scratch_shapes=[
            pltpu.VMEM((units, block, block), bf16),
            pltpu.VMEM((units, block, block), bf16),
            pltpu.VMEM((units, block, block), bf16),
            pltpu.VMEM((ENV_RING, 2, 4, 2, slab, block), bf16),
            pltpu.VMEM((ENV_RING, 2, block, block), bf16),
            pltpu.VMEM((2, block, block), bf16),
            pltpu.VMEM((2, block, block), bf16),
            pltpu.VMEM((units, 4, slab, block), bf16),
            pltpu.VMEM((units, 4, slab, block), bf16),
            pltpu.VMEM((RING, 4, slab, block), f32),
            pltpu.VMEM((2, units, slab // 2, block), bf16),
            pltpu.VMEM((2, units, slab // 2, block), bf16),
            pltpu.VMEM((2, units, slab, block), bf16),
            pltpu.VMEM((2, units, slab, block), bf16),
            pltpu.VMEM((Z_SLOTS, 2, 4, slab, block), f32),
            pltpu.VMEM((2, Z_SLOTS, slab, block), bf16),
            pltpu.VMEM((2, Z_SLOTS, slab, block), bf16),
            pltpu.VMEM((2, Z_SLOTS, 2, slab, block), bf16),
            pltpu.VMEM((2, Z_SLOTS, 2, slab, block), bf16),
            pltpu.VMEM((Z_SLOTS, slab, block), bf16),
            pltpu.VMEM((Z_SLOTS, slab, block), bf16),
            pltpu.VMEM((units, slab, block), bf16),
            pltpu.SemaphoreType.DMA((KINDS, units)),
            pltpu.SemaphoreType.DMA((KINDS, units)),
            pltpu.SemaphoreType.DMA((units,)),
            pltpu.SemaphoreType.DMA((ENV_RING,)),
            pltpu.SemaphoreType.DMA((ENV_RING,)),
            pltpu.SemaphoreType.DMA((units,)),
        ],
        compiler_params=pltpu.CompilerParams(
            collective_id=0, has_side_effects=True, vmem_limit_bytes=66 * 1000 * 1000
        ),
        name="matvec",
    )(mpo_shift, block_dims, wavefunction, left_env, right_env)


def solution(mesh):
    placed = (
        P(None, "sec", None, None),
        P("mpo", "sec", None, None),
        P("mpo", "sec", None, None),
        P("sec"),
        P("mpo"),
    )
    return jax.shard_map(
        body, mesh=mesh, in_specs=placed, out_specs=P(None, "sec", "mpo", None), check_vma=False
    )
```

```python
import functools

import jax
import jax.numpy as jnp
from jax import lax
from jax.experimental import pallas as pl
from jax.experimental.pallas import tpu as pltpu
from jax.sharding import PartitionSpec as P

MESH = pl.DeviceIdType.MESH
LAGS = (2, 4, 6)
TAIL_LAGS = (2, 4, 6)
AHEAD = 2
DRAIN_LAG = max(LAGS + TAIL_LAGS) + 1
RING = max(LAGS) + 1
ENV_RING = 3
BY_QUARTER = (0, 3, 4, 6, 10)
THROUGH_PAIR = (1, 2, 7, 8)
WHOLE = (11, 13, 15)
Z_FIRST = (4, 8, 11, 14)
Z_SLOTS = len(Z_FIRST)
CHIP, SIDE, FWD_UP, FWD_DOWN, HOP_UP, HOP_DOWN, RELAY_UP, RELAY_DOWN, SUM_UP, SUM_DOWN = range(10)
PAIR_FAR, PAIR_ABOVE, PAIR_BELOW, PAIR_OWN, FWD_PAIR = range(10, 15)
KINDS = 15


def one_of(unit, members):
    found = unit == members[0]
    for member in members[1:]:
        found = found | (unit == member)
    return found


def is_tail(unit):
    return one_of(unit, Z_FIRST)


def tail_slot(unit):
    return sum((unit > member).astype(jnp.int32) for member in Z_FIRST[:-1])


def kernel(
    shift_ref, dims_ref, wave_ref, left_ref, right_ref, out_ref,
    own, chip, side, left_buf, right_buf, chosen, parts,
    pair_send, pair_recv, total, relay_send, relay_recv, sum_send, sum_recv,
    tail_total, tail_relay_send, tail_relay_recv, tail_sum_send, tail_sum_recv, tail_pair_send, tail_pair_recv,
    out_buf, send_sem, recv_sem, own_sem, left_sem, right_sem, out_sem,
):
    bf16, f32 = jnp.bfloat16, jnp.float32
    slots, block = wave_ref.shape[1], wave_ref.shape[2]
    units = 2 * slots
    half, quarter, eighth = block // 2, block // 4, block // 8
    slab = block // 8
    mpo = lax.axis_index("mpo")
    sec = lax.axis_index("sec")
    secs = lax.axis_size("sec")
    core = sec % 2
    z = mpo // 2
    x_lo = mpo % 2
    above, below, far = (z + 1) % 4, (z + 3) % 4, (z + 2) % 4
    direct = (z % 2) * half
    indirect = half - direct
    near_mine, near_theirs = direct + x_lo * quarter, direct + (1 - x_lo) * quarter
    off_mine, off_theirs = indirect + x_lo * quarter, indirect + (1 - x_lo) * quarter
    up = ((mpo + 2) % 8, sec)
    down = ((mpo + 6) % 8, sec)
    pair = (mpo + 1 - 2 * x_lo, sec)
    chip_mate = (mpo, sec + 1 - 2 * core)
    side_mate = (mpo + 1 - 2 * x_lo, (sec + secs - 1 + 2 * core) % secs)
    first = (secs - 1 - sec) // (secs - 1)
    last = sec // (secs - 1)

    def remote(kind, unit, src, dst, device):
        return pltpu.make_async_remote_copy(
            src_ref=src, dst_ref=dst, send_sem=send_sem.at[kind, unit],
            recv_sem=recv_sem.at[kind, unit], device_id=device, device_id_type=MESH,
        )

    def chip_copy(unit):
        return remote(CHIP, unit, wave_ref.at[unit % 2, unit // 2], chip.at[unit], chip_mate)

    def side_copy(unit, start, size):
        source = (unit // 2 + first - last + slots) % slots
        rows = pl.ds(start, size)
        return remote(SIDE, unit, wave_ref.at[unit % 2, source, rows], side.at[unit, rows], side_mate)

    def pass_on(kind, unit, start, size, device):
        piece = side.at[unit, pl.ds(start, size)]
        return remote(kind, unit, piece, piece, device)

    def half_up(unit, start):
        return pass_on(FWD_UP, unit, start, quarter, up)

    def half_down(unit, start):
        return pass_on(FWD_DOWN, unit, start + quarter, quarter, down)

    def quarter_up(unit, layer):
        return pass_on(FWD_UP, unit, layer * quarter, quarter, up)

    def quarter_down(unit, layer):
        return pass_on(FWD_DOWN, unit, layer * quarter, quarter, down)

    def hop_up(unit, layer):
        return pass_on(HOP_UP, unit, layer * quarter, eighth, up)

    def hop_down(unit, layer):
        return pass_on(HOP_DOWN, unit, layer * quarter + eighth, eighth, down)

    def pair_copy(kind, unit):
        layer = {PAIR_FAR: far, PAIR_ABOVE: above, PAIR_BELOW: below, PAIR_OWN: z}[kind]
        return remote(kind, unit, pair_send.at[unit, layer], pair_recv.at[unit, layer], pair)

    def relay_copy(way, unit):
        return remote(RELAY_UP + way, unit, relay_send.at[way, unit], relay_recv.at[way, unit], (up, down)[way])

    def sum_copy(way, unit):
        return remote(SUM_UP + way, unit, sum_send.at[way, unit], sum_recv.at[way, unit], (up, down)[way])

    def tail_pair_copy(unit):
        at = tail_slot(unit)
        return remote(PAIR_OWN, unit, tail_pair_send.at[at], tail_pair_recv.at[at], pair)

    def tail_relay_copy(way, unit):
        at = tail_slot(unit)
        return remote(
            RELAY_UP + way, unit, tail_relay_send.at[way, at], tail_relay_recv.at[way, at], (up, down)[way]
        )

    def tail_sum_copy(way, unit):
        at = tail_slot(unit)
        return remote(SUM_UP + way, unit, tail_sum_send.at[way, at], tail_sum_recv.at[way, at], (up, down)[way])

    def own_copy(unit):
        return pltpu.make_async_copy(wave_ref.at[unit % 2, unit // 2], own.at[unit], own_sem.at[unit])

    def out_copy(unit):
        return pltpu.make_async_copy(out_buf.at[unit], out_ref.at[unit % 2, unit // 2], out_sem.at[unit])

    def left_copy(slot):
        at = slot % ENV_RING
        return pltpu.make_async_copy(left_ref.at[:, slot], left_buf.at[at], left_sem.at[at])

    def right_copy(slot):
        at = slot % ENV_RING
        return pltpu.make_async_copy(right_ref.at[:, slot], right_buf.at[at], right_sem.at[at])

    barrier = pltpu.get_barrier_semaphore()
    for mate in (up, down, pair, chip_mate, side_mate):
        pl.semaphore_signal(barrier, inc=1, device_id=mate, device_id_type=MESH)

    def start_local(slot, carry):
        own_copy(2 * slot).start()
        own_copy(2 * slot + 1).start()
        left_copy(slot).start()
        right_copy(slot).start()
        return carry

    lax.fori_loop(0, ENV_RING - 1, start_local, 0)
    pl.semaphore_wait(barrier, 5)

    def by_kind(unit, quarters=None, through=None, whole=None, halves=None):
        kinds = [one_of(unit, members) for members in (BY_QUARTER, THROUGH_PAIR, WHOLE)]
        kinds.append((unit >= 0) & (unit < units) & jnp.logical_not(kinds[0] | kinds[1] | kinds[2]))
        for found, action in zip(kinds, (quarters, through, whole, halves)):
            if action is not None:
                pl.when(found)(action)

    def start_remote(unit, carry):
        by_kind(
            unit,
            lambda: side_copy(unit, z * quarter, quarter).start(),
            lambda: side_copy(unit, near_theirs, quarter).start(),
            lambda: side_copy(unit, 0, block).start(),
            lambda: side_copy(unit, direct, half).start(),
        )
        chip_copy(unit).start()
        return carry

    lax.fori_loop(0, units, start_remote, 0)

    def stage_quarter(unit):
        side_copy(unit, z * quarter, quarter).wait_recv()
        quarter_up(unit, z).start()
        quarter_down(unit, z).start()

    def stage_hop(unit):
        quarter_up(unit, below).wait_recv()
        hop_up(unit, below).start()
        quarter_down(unit, above).wait_recv()
        hop_down(unit, above).start()

    def through_pair(unit, near):
        return [pass_on(FWD_PAIR, unit, near, quarter, pair)]

    def through_forward(unit, near):
        return [
            pass_on(FWD_UP, unit, near, eighth, up),
            pass_on(FWD_DOWN, unit, near + eighth, eighth, down),
        ]

    def through_hop(unit, off):
        return [
            pass_on(HOP_UP, unit, off, eighth, up),
            pass_on(HOP_DOWN, unit, off + eighth, eighth, down),
        ]

    def stage_through(unit):
        side_copy(unit, near_mine, quarter).wait_recv()
        for copy in through_pair(unit, near_mine) + through_forward(unit, near_mine):
            copy.start()

    def stage_through_hop(unit):
        through_pair(unit, near_theirs)[0].wait_recv()
        for copy in through_hop(unit, near_theirs):
            copy.start()

    def stage_half(unit):
        side_copy(unit, direct, half).wait_recv()
        half_up(unit, direct).start()
        half_down(unit, direct).start()

    def write(unit, value):
        limit = dims_ref[unit // 2]
        rows = mpo * slab + lax.broadcasted_iota(jnp.int32, value.shape, 0)
        cols = lax.broadcasted_iota(jnp.int32, value.shape, 1)
        inside = (rows < limit) & (cols < limit)
        out_buf[unit] = jnp.where(inside, value, jnp.zeros_like(value)).astype(bf16)
        out_copy(unit).start()

    top, bottom = pl.ds(0, slab // 2), pl.ds(slab // 2, slab // 2)

    def summed(unit, layer, rows=slice(None)):
        return total[unit % RING, layer, rows] + pair_recv[unit, layer, rows].astype(f32)

    def stage_finish(unit):
        pair_copy(PAIR_OWN, unit).wait_recv()
        sum_copy(0, unit).wait_recv()
        sum_copy(1, unit).wait_recv()
        value = summed(unit, z) + sum_recv[0, unit].astype(f32)
        write(unit, value + sum_recv[1, unit].astype(f32))

    def stage_sum(unit):
        pair_copy(PAIR_ABOVE, unit).wait_recv()
        relay_copy(0, unit).wait_recv()
        sum_send[0, unit, top] = (summed(unit, above, top) + relay_recv[0, unit].astype(f32)).astype(bf16)
        sum_send[0, unit, bottom] = summed(unit, above, bottom).astype(bf16)
        sum_copy(0, unit).start()
        pair_copy(PAIR_BELOW, unit).wait_recv()
        relay_copy(1, unit).wait_recv()
        sum_send[1, unit, top] = summed(unit, below, top).astype(bf16)
        sum_send[1, unit, bottom] = (summed(unit, below, bottom) + relay_recv[1, unit].astype(f32)).astype(bf16)
        sum_copy(1, unit).start()

    def stage_pair(unit):
        pair_copy(PAIR_FAR, unit).wait_recv()
        relay_send[0, unit] = summed(unit, far, top).astype(bf16)
        relay_copy(0, unit).start()
        relay_send[1, unit] = summed(unit, far, bottom).astype(bf16)
        relay_copy(1, unit).start()

    def tail_finish(unit):
        at = tail_slot(unit)
        tail_pair_copy(unit).wait_recv()
        write(unit, tail_total[at, 1, z] + tail_pair_recv[at].astype(f32))

    def tail_pair(unit):
        at = tail_slot(unit)
        tail_sum_copy(0, unit).wait_recv()
        tail_sum_copy(1, unit).wait_recv()
        for side_of in range(2):
            value = tail_total[at, side_of, z] + tail_sum_recv[0, at, side_of].astype(f32)
            value = value + tail_sum_recv[1, at, side_of].astype(f32)
            if side_of == 0:
                tail_pair_send[at] = value.astype(bf16)
                tail_pair_copy(unit).start()
            else:
                tail_total[at, 1, z] = value

    def tail_sum(unit):
        at = tail_slot(unit)
        tail_relay_copy(0, unit).wait_recv()
        tail_sum_send[0, at, 0] = (tail_total[at, 0, above] + tail_relay_recv[0, at].astype(f32)).astype(bf16)
        tail_sum_send[0, at, 1] = tail_total[at, 1, above].astype(bf16)
        tail_sum_copy(0, unit).start()
        tail_relay_copy(1, unit).wait_recv()
        tail_sum_send[1, at, 0] = tail_total[at, 0, below].astype(bf16)
        tail_sum_send[1, at, 1] = (tail_total[at, 1, below] + tail_relay_recv[1, at].astype(f32)).astype(bf16)
        tail_sum_copy(1, unit).start()

    def stage_compute(unit):
        slot = unit // 2
        at = slot % ENV_RING
        own_copy(unit).wait()

        @pl.when(unit % 2 == 0)
        def _():
            left_copy(slot).wait()
            right_copy(slot).wait()

        chip_copy(unit).wait_recv()

        def wait_hops():
            hop_up(unit, far).wait_recv()
            hop_down(unit, far).wait_recv()

        def wait_halves():
            half_up(unit, indirect).wait_recv()
            half_down(unit, indirect).wait_recv()

        def wait_through():
            for copy in through_forward(unit, off_mine) + through_hop(unit, off_theirs):
                copy.wait_recv()

        by_kind(unit, wait_hops, wait_through, lambda: side_copy(unit, 0, block).wait_recv(), wait_halves)

        missing = first * ((slots - 1 - slot) // (slots - 1)) + last * (slot // (slots - 1))
        for w in range(2):
            turn = shift_ref[w] * (1 - 2 * core)
            use_side = (turn == 1).astype(f32) * (1 - missing).astype(f32)
            use_chip = (turn == -1).astype(f32)
            use_own = (turn == 0).astype(f32)
            chosen[w] = (
                own[unit] * use_own.astype(bf16)
                + chip[unit] * use_chip.astype(bf16)
                + side[unit] * use_side.astype(bf16)
            )
            theirs = left_buf[at, w, :, 1 - x_lo].reshape(half, block)
            mine = left_buf[at, w, :, x_lo].reshape(half, block)
            rows = jnp.concatenate([theirs, mine], axis=0)
            parts[w] = jnp.dot(rows, chosen[w], preferred_element_type=f32).astype(bf16)
        both = jnp.dot(parts[0], right_buf[at, 0], preferred_element_type=f32) + jnp.dot(
            parts[1], right_buf[at, 1], preferred_element_type=f32
        )

        @pl.when(jnp.logical_not(is_tail(unit)))
        def _():
            pair_send[unit] = both[:half].astype(bf16).reshape(4, slab, block)
            for kind in (PAIR_FAR, PAIR_ABOVE, PAIR_BELOW, PAIR_OWN):
                pair_copy(kind, unit).start()
            total[unit % RING] = both[half:].reshape(4, slab, block)

        @pl.when(is_tail(unit))
        def _():
            tail = tail_slot(unit)
            tail_total[tail] = both.reshape(2, 4, slab, block)
            for way in range(2):
                tail_relay_send[way, tail] = tail_total[tail, way, far].astype(bf16)
                tail_relay_copy(way, unit).start()

    def drain_quarters(unit):
        side_copy(unit, z * quarter, quarter).wait_send()
        quarter_up(unit, z).wait_send()
        quarter_down(unit, z).wait_send()
        hop_up(unit, below).wait_send()
        hop_down(unit, above).wait_send()

    def drain_through(unit):
        side_copy(unit, near_theirs, quarter).wait_send()
        copies = through_pair(unit, near_mine) + through_forward(unit, near_mine)
        for copy in copies + through_hop(unit, near_theirs):
            copy.wait_send()

    def drain_halves(unit):
        side_copy(unit, direct, half).wait_send()
        half_up(unit, direct).wait_send()
        half_down(unit, direct).wait_send()

    def drain(unit):
        by_kind(
            unit,
            lambda: drain_quarters(unit),
            lambda: drain_through(unit),
            lambda: side_copy(unit, 0, block).wait_send(),
            lambda: drain_halves(unit),
        )
        out_copy(unit).wait()
        chip_copy(unit).wait_send()

        @pl.when(jnp.logical_not(is_tail(unit)))
        def _():
            for kind in (PAIR_FAR, PAIR_ABOVE, PAIR_BELOW, PAIR_OWN):
                pair_copy(kind, unit).wait_send()
            for way in range(2):
                relay_copy(way, unit).wait_send()
                sum_copy(way, unit).wait_send()

        @pl.when(is_tail(unit))
        def _():
            tail_pair_copy(unit).wait_send()
            for way in range(2):
                tail_relay_copy(way, unit).wait_send()
                tail_sum_copy(way, unit).wait_send()

    def step(i, carry):
        now = i - AHEAD
        by_kind(i, lambda: stage_quarter(i), lambda: stage_through(i), None, lambda: stage_half(i))
        ahead = now // 2 + ENV_RING - 1

        @pl.when((now >= 0) & (now % 2 == 0) & (ahead < slots))
        def _():
            start_local(ahead, 0)

        def later(lag, tail, stage):
            unit = now - lag
            kind = is_tail(unit) if tail else jnp.logical_not(is_tail(unit))

            @pl.when((unit >= 0) & (unit < units) & kind)
            def _():
                stage(unit)

        stages = list(zip(LAGS, (False,) * 3, (stage_pair, stage_sum, stage_finish)))
        stages += zip(TAIL_LAGS, (True,) * 3, (tail_sum, tail_pair, tail_finish))
        for lag, tail, stage in sorted(stages, key=lambda item: -item[0]):
            later(lag, tail, stage)

        by_kind(now + 1, lambda: stage_hop(now + 1), lambda: stage_through_hop(now + 1))

        @pl.when((now >= 0) & (now < units))
        def _():
            stage_compute(now)

        done = now - DRAIN_LAG

        @pl.when((done >= 0) & (done < units))
        def _():
            drain(done)

        return carry

    lax.fori_loop(0, AHEAD + units + DRAIN_LAG, step, 0)


def body(wavefunction, left_env, right_env, block_dims, mpo_shift):
    vectors, slots, block, _ = wavefunction.shape
    slab, units = block // 8, 2 * slots
    left_env = left_env.reshape(2, slots, 4, 2, slab, block)
    bf16, f32 = jnp.bfloat16, jnp.float32
    smem = pl.BlockSpec(memory_space=pltpu.SMEM)
    anywhere = pl.BlockSpec(memory_space=pl.ANY)
    return pl.pallas_call(
        kernel,
        out_shape=jax.ShapeDtypeStruct((vectors, slots, slab, block), bf16),
        in_specs=[smem, smem, anywhere, anywhere, anywhere],
        out_specs=anywhere,
        scratch_shapes=[
            pltpu.VMEM((units, block, block), bf16),
            pltpu.VMEM((units, block, block), bf16),
            pltpu.VMEM((units, block, block), bf16),
            pltpu.VMEM((ENV_RING, 2, 4, 2, slab, block), bf16),
            pltpu.VMEM((ENV_RING, 2, block, block), bf16),
            pltpu.VMEM((2, block, block), bf16),
            pltpu.VMEM((2, block, block), bf16),
            pltpu.VMEM((units, 4, slab, block), bf16),
            pltpu.VMEM((units, 4, slab, block), bf16),
            pltpu.VMEM((RING, 4, slab, block), f32),
            pltpu.VMEM((2, units, slab // 2, block), bf16),
            pltpu.VMEM((2, units, slab // 2, block), bf16),
            pltpu.VMEM((2, units, slab, block), bf16),
            pltpu.VMEM((2, units, slab, block), bf16),
            pltpu.VMEM((Z_SLOTS, 2, 4, slab, block), f32),
            pltpu.VMEM((2, Z_SLOTS, slab, block), bf16),
            pltpu.VMEM((2, Z_SLOTS, slab, block), bf16),
            pltpu.VMEM((2, Z_SLOTS, 2, slab, block), bf16),
            pltpu.VMEM((2, Z_SLOTS, 2, slab, block), bf16),
            pltpu.VMEM((Z_SLOTS, slab, block), bf16),
            pltpu.VMEM((Z_SLOTS, slab, block), bf16),
            pltpu.VMEM((units, slab, block), bf16),
            pltpu.SemaphoreType.DMA((KINDS, units)),
            pltpu.SemaphoreType.DMA((KINDS, units)),
            pltpu.SemaphoreType.DMA((units,)),
            pltpu.SemaphoreType.DMA((ENV_RING,)),
            pltpu.SemaphoreType.DMA((ENV_RING,)),
            pltpu.SemaphoreType.DMA((units,)),
        ],
        compiler_params=pltpu.CompilerParams(
            collective_id=0, has_side_effects=True, vmem_limit_bytes=66 * 1000 * 1000
        ),
        name="matvec",
    )(mpo_shift, block_dims, wavefunction, left_env, right_env)


def solution(mesh):
    placed = (
        P(None, "sec", None, None),
        P("mpo", "sec", None, None),
        P("mpo", "sec", None, None),
        P("sec"),
        P("mpo"),
    )
    return jax.shard_map(
        body, mesh=mesh, in_specs=placed, out_specs=P(None, "sec", "mpo", None), check_vma=False
    )
```

```python
import functools

import jax
import jax.numpy as jnp
from jax import lax
from jax.experimental import pallas as pl
from jax.experimental.pallas import tpu as pltpu
from jax.sharding import PartitionSpec as P

MESH = pl.DeviceIdType.MESH
LAGS = (2, 4, 6)
TAIL_LAGS = (2, 4, 6)
AHEAD = 2
DRAIN_LAG = max(LAGS + TAIL_LAGS) + 1
RING = max(LAGS) + 1
ENV_RING = 3
BY_QUARTER = (3, 4)
THROUGH_PAIR = (0, 1, 2, 6, 7)
WHOLE = (14, 15)
Z_FIRST = (3, 7, 11, 14)
Z_SLOTS = len(Z_FIRST)
CHIP, SIDE, FWD_UP, FWD_DOWN, HOP_UP, HOP_DOWN, RELAY_UP, RELAY_DOWN, SUM_UP, SUM_DOWN = range(10)
PAIR_FAR, PAIR_ABOVE, PAIR_BELOW, PAIR_OWN, FWD_PAIR = range(10, 15)
KINDS = 15


def one_of(unit, members):
    found = unit == members[0]
    for member in members[1:]:
        found = found | (unit == member)
    return found


def is_tail(unit):
    return one_of(unit, Z_FIRST)


def tail_slot(unit):
    return sum((unit > member).astype(jnp.int32) for member in Z_FIRST[:-1])


def kernel(
    shift_ref, dims_ref, wave_ref, left_ref, right_ref, out_ref,
    own, chip, side, left_buf, right_buf, chosen, parts,
    pair_send, pair_recv, total, relay_send, relay_recv, sum_send, sum_recv,
    tail_total, tail_relay_send, tail_relay_recv, tail_sum_send, tail_sum_recv, tail_pair_send, tail_pair_recv,
    out_buf, send_sem, recv_sem, own_sem, left_sem, right_sem, out_sem,
):
    bf16, f32 = jnp.bfloat16, jnp.float32
    slots, block = wave_ref.shape[1], wave_ref.shape[2]
    units = 2 * slots
    half, quarter, eighth = block // 2, block // 4, block // 8
    slab = block // 8
    mpo = lax.axis_index("mpo")
    sec = lax.axis_index("sec")
    secs = lax.axis_size("sec")
    core = sec % 2
    z = mpo // 2
    x_lo = mpo % 2
    above, below, far = (z + 1) % 4, (z + 3) % 4, (z + 2) % 4
    direct = (z % 2) * half
    indirect = half - direct
    near_mine, near_theirs = direct + x_lo * quarter, direct + (1 - x_lo) * quarter
    off_mine, off_theirs = indirect + x_lo * quarter, indirect + (1 - x_lo) * quarter
    up = ((mpo + 2) % 8, sec)
    down = ((mpo + 6) % 8, sec)
    pair = (mpo + 1 - 2 * x_lo, sec)
    chip_mate = (mpo, sec + 1 - 2 * core)
    side_mate = (mpo + 1 - 2 * x_lo, (sec + secs - 1 + 2 * core) % secs)
    first = (secs - 1 - sec) // (secs - 1)
    last = sec // (secs - 1)

    def remote(kind, unit, src, dst, device):
        return pltpu.make_async_remote_copy(
            src_ref=src, dst_ref=dst, send_sem=send_sem.at[kind, unit],
            recv_sem=recv_sem.at[kind, unit], device_id=device, device_id_type=MESH,
        )

    def chip_copy(unit):
        return remote(CHIP, unit, wave_ref.at[unit % 2, unit // 2], chip.at[unit], chip_mate)

    def side_copy(unit, start, size):
        source = (unit // 2 + first - last + slots) % slots
        rows = pl.ds(start, size)
        return remote(SIDE, unit, wave_ref.at[unit % 2, source, rows], side.at[unit, rows], side_mate)

    def pass_on(kind, unit, start, size, device):
        piece = side.at[unit, pl.ds(start, size)]
        return remote(kind, unit, piece, piece, device)

    def half_up(unit, start):
        return pass_on(FWD_UP, unit, start, quarter, up)

    def half_down(unit, start):
        return pass_on(FWD_DOWN, unit, start + quarter, quarter, down)

    def quarter_up(unit, layer):
        return pass_on(FWD_UP, unit, layer * quarter, quarter, up)

    def quarter_down(unit, layer):
        return pass_on(FWD_DOWN, unit, layer * quarter, quarter, down)

    def hop_up(unit, layer):
        return pass_on(HOP_UP, unit, layer * quarter, eighth, up)

    def hop_down(unit, layer):
        return pass_on(HOP_DOWN, unit, layer * quarter + eighth, eighth, down)

    def pair_copy(kind, unit):
        layer = {PAIR_FAR: far, PAIR_ABOVE: above, PAIR_BELOW: below, PAIR_OWN: z}[kind]
        return remote(kind, unit, pair_send.at[unit, layer], pair_recv.at[unit, layer], pair)

    def relay_copy(way, unit):
        return remote(RELAY_UP + way, unit, relay_send.at[way, unit], relay_recv.at[way, unit], (up, down)[way])

    def sum_copy(way, unit):
        return remote(SUM_UP + way, unit, sum_send.at[way, unit], sum_recv.at[way, unit], (up, down)[way])

    def tail_pair_copy(unit):
        at = tail_slot(unit)
        return remote(PAIR_OWN, unit, tail_pair_send.at[at], tail_pair_recv.at[at], pair)

    def tail_relay_copy(way, unit):
        at = tail_slot(unit)
        return remote(
            RELAY_UP + way, unit, tail_relay_send.at[way, at], tail_relay_recv.at[way, at], (up, down)[way]
        )

    def tail_sum_copy(way, unit):
        at = tail_slot(unit)
        return remote(SUM_UP + way, unit, tail_sum_send.at[way, at], tail_sum_recv.at[way, at], (up, down)[way])

    def own_copy(unit):
        return pltpu.make_async_copy(wave_ref.at[unit % 2, unit // 2], own.at[unit], own_sem.at[unit])

    def out_copy(unit):
        return pltpu.make_async_copy(out_buf.at[unit], out_ref.at[unit % 2, unit // 2], out_sem.at[unit])

    def left_copy(slot):
        at = slot % ENV_RING
        return pltpu.make_async_copy(left_ref.at[:, slot], left_buf.at[at], left_sem.at[at])

    def right_copy(slot):
        at = slot % ENV_RING
        return pltpu.make_async_copy(right_ref.at[:, slot], right_buf.at[at], right_sem.at[at])

    barrier = pltpu.get_barrier_semaphore()
    for mate in (up, down, pair, chip_mate, side_mate):
        pl.semaphore_signal(barrier, inc=1, device_id=mate, device_id_type=MESH)

    def start_local(slot, carry):
        own_copy(2 * slot).start()
        own_copy(2 * slot + 1).start()
        left_copy(slot).start()
        right_copy(slot).start()
        return carry

    lax.fori_loop(0, ENV_RING - 1, start_local, 0)
    pl.semaphore_wait(barrier, 5)

    def by_kind(unit, quarters=None, through=None, whole=None, halves=None):
        kinds = [one_of(unit, members) for members in (BY_QUARTER, THROUGH_PAIR, WHOLE)]
        kinds.append((unit >= 0) & (unit < units) & jnp.logical_not(kinds[0] | kinds[1] | kinds[2]))
        for found, action in zip(kinds, (quarters, through, whole, halves)):
            if action is not None:
                pl.when(found)(action)

    def start_remote(unit, carry):
        by_kind(
            unit,
            lambda: side_copy(unit, z * quarter, quarter).start(),
            lambda: side_copy(unit, near_theirs, quarter).start(),
            lambda: side_copy(unit, 0, block).start(),
            lambda: side_copy(unit, direct, half).start(),
        )
        chip_copy(unit).start()
        return carry

    lax.fori_loop(0, units, start_remote, 0)

    def stage_quarter(unit):
        side_copy(unit, z * quarter, quarter).wait_recv()
        quarter_up(unit, z).start()
        quarter_down(unit, z).start()

    def stage_hop(unit):
        quarter_up(unit, below).wait_recv()
        hop_up(unit, below).start()
        quarter_down(unit, above).wait_recv()
        hop_down(unit, above).start()

    def through_pair(unit, near):
        return [pass_on(FWD_PAIR, unit, near, quarter, pair)]

    def through_forward(unit, near):
        return [
            pass_on(FWD_UP, unit, near, eighth, up),
            pass_on(FWD_DOWN, unit, near + eighth, eighth, down),
        ]

    def through_hop(unit, off):
        return [
            pass_on(HOP_UP, unit, off, eighth, up),
            pass_on(HOP_DOWN, unit, off + eighth, eighth, down),
        ]

    def stage_through(unit):
        side_copy(unit, near_mine, quarter).wait_recv()
        for copy in through_pair(unit, near_mine) + through_forward(unit, near_mine):
            copy.start()

    def stage_through_hop(unit):
        through_pair(unit, near_theirs)[0].wait_recv()
        for copy in through_hop(unit, near_theirs):
            copy.start()

    def stage_half(unit):
        side_copy(unit, direct, half).wait_recv()
        half_up(unit, direct).start()
        half_down(unit, direct).start()

    def write(unit, value):
        limit = dims_ref[unit // 2]
        rows = mpo * slab + lax.broadcasted_iota(jnp.int32, value.shape, 0)
        cols = lax.broadcasted_iota(jnp.int32, value.shape, 1)
        inside = (rows < limit) & (cols < limit)
        out_buf[unit] = jnp.where(inside, value, jnp.zeros_like(value)).astype(bf16)
        out_copy(unit).start()

    top, bottom = pl.ds(0, slab // 2), pl.ds(slab // 2, slab // 2)

    def summed(unit, layer, rows=slice(None)):
        return total[unit % RING, layer, rows] + pair_recv[unit, layer, rows].astype(f32)

    def stage_finish(unit):
        pair_copy(PAIR_OWN, unit).wait_recv()
        sum_copy(0, unit).wait_recv()
        sum_copy(1, unit).wait_recv()
        value = summed(unit, z) + sum_recv[0, unit].astype(f32)
        write(unit, value + sum_recv[1, unit].astype(f32))

    def stage_sum(unit):
        pair_copy(PAIR_ABOVE, unit).wait_recv()
        relay_copy(0, unit).wait_recv()
        sum_send[0, unit, top] = (summed(unit, above, top) + relay_recv[0, unit].astype(f32)).astype(bf16)
        sum_send[0, unit, bottom] = summed(unit, above, bottom).astype(bf16)
        sum_copy(0, unit).start()
        pair_copy(PAIR_BELOW, unit).wait_recv()
        relay_copy(1, unit).wait_recv()
        sum_send[1, unit, top] = summed(unit, below, top).astype(bf16)
        sum_send[1, unit, bottom] = (summed(unit, below, bottom) + relay_recv[1, unit].astype(f32)).astype(bf16)
        sum_copy(1, unit).start()

    def stage_pair(unit):
        pair_copy(PAIR_FAR, unit).wait_recv()
        relay_send[0, unit] = summed(unit, far, top).astype(bf16)
        relay_copy(0, unit).start()
        relay_send[1, unit] = summed(unit, far, bottom).astype(bf16)
        relay_copy(1, unit).start()

    def tail_finish(unit):
        at = tail_slot(unit)
        tail_pair_copy(unit).wait_recv()
        write(unit, tail_total[at, 1, z] + tail_pair_recv[at].astype(f32))

    def tail_pair(unit):
        at = tail_slot(unit)
        tail_sum_copy(0, unit).wait_recv()
        tail_sum_copy(1, unit).wait_recv()
        for side_of in range(2):
            value = tail_total[at, side_of, z] + tail_sum_recv[0, at, side_of].astype(f32)
            value = value + tail_sum_recv[1, at, side_of].astype(f32)
            if side_of == 0:
                tail_pair_send[at] = value.astype(bf16)
                tail_pair_copy(unit).start()
            else:
                tail_total[at, 1, z] = value

    def tail_sum(unit):
        at = tail_slot(unit)
        tail_relay_copy(0, unit).wait_recv()
        tail_sum_send[0, at, 0] = (tail_total[at, 0, above] + tail_relay_recv[0, at].astype(f32)).astype(bf16)
        tail_sum_send[0, at, 1] = tail_total[at, 1, above].astype(bf16)
        tail_sum_copy(0, unit).start()
        tail_relay_copy(1, unit).wait_recv()
        tail_sum_send[1, at, 0] = tail_total[at, 0, below].astype(bf16)
        tail_sum_send[1, at, 1] = (tail_total[at, 1, below] + tail_relay_recv[1, at].astype(f32)).astype(bf16)
        tail_sum_copy(1, unit).start()

    def stage_compute(unit):
        slot = unit // 2
        at = slot % ENV_RING
        own_copy(unit).wait()

        @pl.when(unit % 2 == 0)
        def _():
            left_copy(slot).wait()
            right_copy(slot).wait()

        chip_copy(unit).wait_recv()

        def wait_hops():
            hop_up(unit, far).wait_recv()
            hop_down(unit, far).wait_recv()

        def wait_halves():
            half_up(unit, indirect).wait_recv()
            half_down(unit, indirect).wait_recv()

        def wait_through():
            for copy in through_forward(unit, off_mine) + through_hop(unit, off_theirs):
                copy.wait_recv()

        by_kind(unit, wait_hops, wait_through, lambda: side_copy(unit, 0, block).wait_recv(), wait_halves)

        missing = first * ((slots - 1 - slot) // (slots - 1)) + last * (slot // (slots - 1))
        for w in range(2):
            turn = shift_ref[w] * (1 - 2 * core)
            use_side = (turn == 1).astype(f32) * (1 - missing).astype(f32)
            use_chip = (turn == -1).astype(f32)
            use_own = (turn == 0).astype(f32)
            chosen[w] = (
                own[unit] * use_own.astype(bf16)
                + chip[unit] * use_chip.astype(bf16)
                + side[unit] * use_side.astype(bf16)
            )
            theirs = left_buf[at, w, :, 1 - x_lo].reshape(half, block)
            mine = left_buf[at, w, :, x_lo].reshape(half, block)
            rows = jnp.concatenate([theirs, mine], axis=0)
            parts[w] = jnp.dot(rows, chosen[w], preferred_element_type=f32).astype(bf16)
        both = jnp.dot(parts[0], right_buf[at, 0], preferred_element_type=f32) + jnp.dot(
            parts[1], right_buf[at, 1], preferred_element_type=f32
        )

        @pl.when(jnp.logical_not(is_tail(unit)))
        def _():
            pair_send[unit] = both[:half].astype(bf16).reshape(4, slab, block)
            for kind in (PAIR_FAR, PAIR_ABOVE, PAIR_BELOW, PAIR_OWN):
                pair_copy(kind, unit).start()
            total[unit % RING] = both[half:].reshape(4, slab, block)

        @pl.when(is_tail(unit))
        def _():
            tail = tail_slot(unit)
            tail_total[tail] = both.reshape(2, 4, slab, block)
            for way in range(2):
                tail_relay_send[way, tail] = tail_total[tail, way, far].astype(bf16)
                tail_relay_copy(way, unit).start()

    def drain_quarters(unit):
        side_copy(unit, z * quarter, quarter).wait_send()
        quarter_up(unit, z).wait_send()
        quarter_down(unit, z).wait_send()
        hop_up(unit, below).wait_send()
        hop_down(unit, above).wait_send()

    def drain_through(unit):
        side_copy(unit, near_theirs, quarter).wait_send()
        copies = through_pair(unit, near_mine) + through_forward(unit, near_mine)
        for copy in copies + through_hop(unit, near_theirs):
            copy.wait_send()

    def drain_halves(unit):
        side_copy(unit, direct, half).wait_send()
        half_up(unit, direct).wait_send()
        half_down(unit, direct).wait_send()

    def drain(unit):
        by_kind(
            unit,
            lambda: drain_quarters(unit),
            lambda: drain_through(unit),
            lambda: side_copy(unit, 0, block).wait_send(),
            lambda: drain_halves(unit),
        )
        out_copy(unit).wait()
        chip_copy(unit).wait_send()

        @pl.when(jnp.logical_not(is_tail(unit)))
        def _():
            for kind in (PAIR_FAR, PAIR_ABOVE, PAIR_BELOW, PAIR_OWN):
                pair_copy(kind, unit).wait_send()
            for way in range(2):
                relay_copy(way, unit).wait_send()
                sum_copy(way, unit).wait_send()

        @pl.when(is_tail(unit))
        def _():
            tail_pair_copy(unit).wait_send()
            for way in range(2):
                tail_relay_copy(way, unit).wait_send()
                tail_sum_copy(way, unit).wait_send()

    def step(i, carry):
        now = i - AHEAD
        by_kind(i, lambda: stage_quarter(i), lambda: stage_through(i), None, lambda: stage_half(i))
        ahead = now // 2 + ENV_RING - 1

        @pl.when((now >= 0) & (now % 2 == 0) & (ahead < slots))
        def _():
            start_local(ahead, 0)

        def later(lag, tail, stage):
            unit = now - lag
            kind = is_tail(unit) if tail else jnp.logical_not(is_tail(unit))

            @pl.when((unit >= 0) & (unit < units) & kind)
            def _():
                stage(unit)

        stages = list(zip(LAGS, (False,) * 3, (stage_pair, stage_sum, stage_finish)))
        stages += zip(TAIL_LAGS, (True,) * 3, (tail_sum, tail_pair, tail_finish))
        for lag, tail, stage in sorted(stages, key=lambda item: -item[0]):
            later(lag, tail, stage)

        by_kind(now + 1, lambda: stage_hop(now + 1), lambda: stage_through_hop(now + 1))

        @pl.when((now >= 0) & (now < units))
        def _():
            stage_compute(now)

        done = now - DRAIN_LAG

        @pl.when((done >= 0) & (done < units))
        def _():
            drain(done)

        return carry

    lax.fori_loop(0, AHEAD + units + DRAIN_LAG, step, 0)


def body(wavefunction, left_env, right_env, block_dims, mpo_shift):
    vectors, slots, block, _ = wavefunction.shape
    slab, units = block // 8, 2 * slots
    left_env = left_env.reshape(2, slots, 4, 2, slab, block)
    bf16, f32 = jnp.bfloat16, jnp.float32
    smem = pl.BlockSpec(memory_space=pltpu.SMEM)
    anywhere = pl.BlockSpec(memory_space=pl.ANY)
    return pl.pallas_call(
        kernel,
        out_shape=jax.ShapeDtypeStruct((vectors, slots, slab, block), bf16),
        in_specs=[smem, smem, anywhere, anywhere, anywhere],
        out_specs=anywhere,
        scratch_shapes=[
            pltpu.VMEM((units, block, block), bf16),
            pltpu.VMEM((units, block, block), bf16),
            pltpu.VMEM((units, block, block), bf16),
            pltpu.VMEM((ENV_RING, 2, 4, 2, slab, block), bf16),
            pltpu.VMEM((ENV_RING, 2, block, block), bf16),
            pltpu.VMEM((2, block, block), bf16),
            pltpu.VMEM((2, block, block), bf16),
            pltpu.VMEM((units, 4, slab, block), bf16),
            pltpu.VMEM((units, 4, slab, block), bf16),
            pltpu.VMEM((RING, 4, slab, block), f32),
            pltpu.VMEM((2, units, slab // 2, block), bf16),
            pltpu.VMEM((2, units, slab // 2, block), bf16),
            pltpu.VMEM((2, units, slab, block), bf16),
            pltpu.VMEM((2, units, slab, block), bf16),
            pltpu.VMEM((Z_SLOTS, 2, 4, slab, block), f32),
            pltpu.VMEM((2, Z_SLOTS, slab, block), bf16),
            pltpu.VMEM((2, Z_SLOTS, slab, block), bf16),
            pltpu.VMEM((2, Z_SLOTS, 2, slab, block), bf16),
            pltpu.VMEM((2, Z_SLOTS, 2, slab, block), bf16),
            pltpu.VMEM((Z_SLOTS, slab, block), bf16),
            pltpu.VMEM((Z_SLOTS, slab, block), bf16),
            pltpu.VMEM((units, slab, block), bf16),
            pltpu.SemaphoreType.DMA((KINDS, units)),
            pltpu.SemaphoreType.DMA((KINDS, units)),
            pltpu.SemaphoreType.DMA((units,)),
            pltpu.SemaphoreType.DMA((ENV_RING,)),
            pltpu.SemaphoreType.DMA((ENV_RING,)),
            pltpu.SemaphoreType.DMA((units,)),
        ],
        compiler_params=pltpu.CompilerParams(
            collective_id=0, has_side_effects=True, vmem_limit_bytes=66 * 1000 * 1000
        ),
        name="matvec",
    )(mpo_shift, block_dims, wavefunction, left_env, right_env)


def solution(mesh):
    placed = (
        P(None, "sec", None, None),
        P("mpo", "sec", None, None),
        P("mpo", "sec", None, None),
        P("sec"),
        P("mpo"),
    )
    return jax.shard_map(
        body, mesh=mesh, in_specs=placed, out_specs=P(None, "sec", "mpo", None), check_vma=False
    )
```
